256 devices in a mesh: rad: 8 (over x_hi, y), azi: 32 (over x_lo, z, core).
Axes of the slice: x: 4 (x_hi: 2, x_lo: 2; x = x_hi * 2 + x_lo), y: 4, z: 8, core: 2. Of those that a mesh axis runs over, the one named last changes fastest.
Arguments:
- tokens: bfloat16 [64, 512, 8, 512], P('rad', 'azi'), may hold values from -6 to 6
- cotangent: bfloat16 [64, 512, 8, 512], P('rad', 'azi'), may hold values from -6 to 6
- ln_gain: float32 [512], replicated, may hold values from 0.5 to 1.5
- qkv_weight: bfloat16 [512, 1536], P('azi'), may hold values from -2 to 2
- out_weight: bfloat16 [512, 512], P('azi'), may hold values from -0.25 to 0.25
- shear_offset: int32 [1], replicated, may hold values from 0 to 511
- window_shift: int32 [3], replicated, may hold values from 1 to 7, as said below
Outputs:
- block_out: bfloat16 [64, 512, 8, 512], P('rad', 'azi')
- grad_tokens: bfloat16 [64, 512, 8, 512], P('rad', 'azi')
- grad_qkv: float32 [512, 1536], P('azi')
- grad_out: float32 [512, 512], P('azi')
- grad_gain: float32 [512], replicated
The draws below stay inside these ranges and needn't reach their ends.
Inputs may be any that keep to these rules, and one draw needn't show every extreme that they name: `window_shift`: the radial entry lies in 1 to 3; the azimuthal and vertical entries lie in 1 to 7, and one of these two equals 7.
All inputs are finite; a program needn't handle non-finite values.
Results may differ from the reference program's by a relative error of at most 0.025.
Values may be sent and summed in bfloat16 or wider, within the bound.
A program may use at most 192 MiB of HBM per device.

```python
import jax
import jax.numpy as jnp
from jax import lax

D = 512
HEADS = 16
HD = 32
WR = 4
WA = 8
WZ = 8
NR = 64
NA = 512
NZ = 8
TOKENS = 262144


def draw_qkv_weight(key, part):
    first_key = jax.random.fold_in(jax.random.fold_in(key, 11), 0)
    drawn = jax.random.normal(first_key, (D, 3 * D), jnp.float32) / D ** 0.5
    return jnp.clip(drawn, -2.0, 2.0).astype(jnp.bfloat16)


def draw_window_shift(key, part):
    first_key, second_key, third_key, fourth_key = jax.random.split(jax.random.fold_in(key, 23), 4)
    radial = jax.random.randint(first_key, (1,), 1, WR)
    azimuthal = jax.random.randint(second_key, (1,), 1, WA)
    vertical = jax.random.randint(third_key, (1,), 1, WZ)
    picker = jax.random.randint(fourth_key, (1,), 0, 2)
    azimuthal = jnp.where(picker == 1, WA - 1, azimuthal)
    vertical = jnp.where(picker == 0, WZ - 1, vertical)
    return jnp.concatenate([radial, azimuthal, vertical]).astype(jnp.int32)


def raised(result, stream_key, source, target, blocks, factor):
    def block_of(axis_at):
        return (jnp.arange(result.shape[axis_at]) // (result.shape[axis_at] // blocks)).reshape((-1,) + (1,) * (result.ndim - 1 - axis_at))

    first = jax.random.permutation(stream_key, blocks)[block_of(target)]
    second = (block_of(target) + blocks // 2) % blocks
    return jnp.where((block_of(source) == first) | (block_of(source) == second), factor * result, result)


def level_of(own_key, extent, cuts, low, largest):
    factor_of, own = 1.0, jax.random.fold_in(own_key, 6)
    for axis_at, blocks in cuts:
        steps = jnp.exp(jax.random.uniform(jax.random.fold_in(own, axis_at), (blocks,), jnp.float32, low / len(cuts), largest / len(cuts)))
        factor_of = factor_of * jnp.repeat(steps, extent[axis_at] // blocks).reshape([-1 if axis == axis_at else 1 for axis in range(len(extent))])
    return factor_of


def bell_draw(rng, shape, deviation, limit, shards=(), held_as=jnp.bfloat16):
    values = jax.random.normal(rng, shape, jnp.float32) * deviation
    if len(shards) > 0:
        values = level_of(rng, shape, shards, -0.22, 0.18) * values
    return jnp.clip(values, min=-limit, max=limit).astype(held_as)


def gaussian_with(key, shape, deviation, limit, pieces, heavy, kind=jnp.bfloat16):
    drawn = deviation * jax.random.normal(key, shape, jnp.float32)
    if pieces:
        drawn = drawn * level_of(key, shape, pieces, -0.22, 0.18)
    return jnp.clip(raised(drawn, jax.random.fold_in(key, 3), *heavy), -limit, limit).astype(kind)


def setup_inputs(seed: int = 0) -> dict:
    key_of = jax.random.split(jax.random.key(seed), 8)
    tokens = gaussian_with(key_of[0], (NR, NA, NZ, D), 1.0, 6.0, ((0, 8), (1, 32)), (1, 3, 32, 2.75))
    cotangent = bell_draw(key_of[1], (NR, NA, NZ, D), 1.0, 6.0, ((0, 8), (1, 32)))
    ln_gain = jnp.clip(1.0 + 0.1 * jax.random.normal(key_of[2], (D,), jnp.float32), 0.5, 1.5)
    qkv_weight = draw_qkv_weight(jax.random.fold_in(key_of[7], 71), 0)
    out_weight = bell_draw(key_of[4], (D, D), D ** -0.5, 0.25, ((0, 32),))
    shear_offset = jax.random.randint(key_of[5], (1,), 0, NA).astype(jnp.int32)
    window_shift = draw_window_shift(jax.random.fold_in(key_of[7], 71), 0)
    return {"tokens": tokens, "cotangent": cotangent, "ln_gain": ln_gain, "qkv_weight": qkv_weight, "out_weight": out_weight, "shear_offset": shear_offset, "window_shift": window_shift}


EPS = 1e-05

def to_windows(tensor, parts):
    extent_r, extent_a, extent_z, channels = tensor.shape
    tensor = tensor.reshape(extent_r // WR, WR, extent_a // WA, WA, extent_z // WZ, WZ, parts, HEADS, HD)
    tensor = tensor.transpose(0, 2, 4, 6, 7, 1, 3, 5, 8)
    return tensor.reshape(-1, parts, HEADS, WR * WA * WZ, HD)

def from_windows(windows, extent_r, extent_a, extent_z):
    parts = windows.shape[1]
    windows = windows.reshape(extent_r // WR, extent_a // WA, extent_z // WZ, parts, HEADS, WR, WA, WZ, HD)
    windows = windows.transpose(0, 5, 1, 6, 2, 7, 3, 4, 8)
    return windows.reshape(extent_r, extent_a, extent_z, parts * HEADS * HD)

def block_pass(shifted, grad_in, ln_gain, qkv_weight, out_weight):
    extent_r, extent_a, extent_z, width = shifted.shape
    number = extent_r * extent_a * extent_z
    contract = (((0,), (0,)), ((), ()))
    scaling = HD ** (-0.5)
    inputs_f = shifted.astype(jnp.float32).reshape(number, width)
    centre = lax.optimization_barrier(jnp.mean(inputs_f, axis=1, keepdims=True))
    centred = inputs_f - centre
    variance = lax.optimization_barrier(jnp.mean(centred * centred, axis=1, keepdims=True))
    inverse_std = lax.rsqrt(variance + EPS)
    normed = centred * inverse_std
    hidden = (normed * ln_gain).astype(jnp.bfloat16)
    qkv = jnp.dot(hidden, qkv_weight, preferred_element_type=jnp.float32).astype(jnp.bfloat16)
    qkv = lax.optimization_barrier(qkv)
    windows = to_windows(qkv.reshape(extent_r, extent_a, extent_z, 3 * width), 3).astype(jnp.float32)
    queries, keys_win, values = (windows[:, 0], windows[:, 1], windows[:, 2])
    scores = jnp.einsum('nhqd,nhkd->nhqk', queries, keys_win) * scaling
    weights = jax.nn.softmax(scores, axis=-1)
    weights_low = lax.optimization_barrier(weights.astype(jnp.bfloat16))
    weights_lf = weights_low.astype(jnp.float32)
    mixed = jnp.einsum('nhqk,nhkd->nhqd', weights_lf, values).astype(jnp.bfloat16)
    attended = from_windows(mixed[:, None], extent_r, extent_a, extent_z).reshape(number, width)
    branch = jnp.dot(attended, out_weight, preferred_element_type=jnp.float32)
    out_shifted = (inputs_f + branch).astype(jnp.bfloat16)
    grad_low = grad_in.reshape(number, width)
    d_attended = jnp.dot(grad_low, out_weight.T, preferred_element_type=jnp.float32).astype(jnp.bfloat16)
    d_attended = lax.optimization_barrier(d_attended)
    d_windows = to_windows(d_attended.reshape(extent_r, extent_a, extent_z, width), 1)[:, 0].astype(jnp.float32)
    d_weights = jnp.einsum('nhqd,nhkd->nhqk', d_windows, values)
    d_values = jnp.einsum('nhqk,nhqd->nhkd', weights_lf, d_windows)
    d_scores = weights * (d_weights - lax.optimization_barrier(jnp.sum(weights * d_weights, axis=-1, keepdims=True)))
    d_scores = lax.optimization_barrier(d_scores.astype(jnp.bfloat16)).astype(jnp.float32)
    d_queries = jnp.einsum('nhqk,nhkd->nhqd', d_scores, keys_win) * scaling
    d_keys = jnp.einsum('nhqk,nhqd->nhkd', d_scores, queries) * scaling
    d_stack = jnp.stack([d_queries, d_keys, d_values], axis=1).astype(jnp.bfloat16)
    d_qkv = from_windows(d_stack, extent_r, extent_a, extent_z).reshape(number, 3 * width)
    d_hidden = jnp.dot(d_qkv, qkv_weight.T, preferred_element_type=jnp.float32)
    grad_qkv = lax.dot_general(hidden, d_qkv, contract, preferred_element_type=jnp.float32)
    grad_out = lax.dot_general(attended, grad_low, contract, preferred_element_type=jnp.float32)
    grad_gain = lax.optimization_barrier(jnp.sum(d_hidden * normed, axis=0))
    d_normed = d_hidden * ln_gain
    d_branch = inverse_std * (d_normed - lax.optimization_barrier(jnp.mean(d_normed, axis=1, keepdims=True)) - normed * lax.optimization_barrier(jnp.mean(d_normed * normed, axis=1, keepdims=True)))
    grad_shifted = (grad_low.astype(jnp.float32) + d_branch).astype(jnp.bfloat16)
    shape_out = (extent_r, extent_a, extent_z, width)
    return (out_shifted.reshape(shape_out), grad_shifted.reshape(shape_out), grad_qkv, grad_out, grad_gain)

def reference(tokens, cotangent, ln_gain, qkv_weight, out_weight, shear_offset, window_shift):
    shift_rad = window_shift[0]
    shift_azi = window_shift[1]
    shift_ver = window_shift[2]
    offset = shear_offset[0]
    rows_fwd = jnp.arange(NR, dtype=jnp.int32) + shift_rad
    wrap_fwd = (rows_fwd >= NR).astype(jnp.int32)
    rows_fwd = rows_fwd % NR
    cols_fwd = (jnp.arange(NA, dtype=jnp.int32)[None, :] + shift_azi + offset * wrap_fwd[:, None]) % NA
    levels_fwd = (jnp.arange(NZ, dtype=jnp.int32) + shift_ver) % NZ
    shifted = tokens[rows_fwd[:, None], cols_fwd][:, :, levels_fwd]
    grad_shift = cotangent[rows_fwd[:, None], cols_fwd][:, :, levels_fwd]
    blocks = NR // WR
    shifted = shifted.reshape(blocks, WR, NA, NZ, D)
    grad_shift = grad_shift.reshape(blocks, WR, NA, NZ, D)

    def scan_step(totals, block_pair):
        out_block, grad_block, term_qkv, term_out, term_gain = block_pass(block_pair[0], block_pair[1], ln_gain, qkv_weight, out_weight)
        return ((totals[0] + term_qkv, totals[1] + term_out, totals[2] + term_gain), (out_block, grad_block))
    start = (jnp.zeros((D, 3 * D), jnp.float32), jnp.zeros((D, D), jnp.float32), jnp.zeros((D,), jnp.float32))
    totals, outputs = lax.scan(scan_step, start, (shifted, grad_shift))
    out_shifted = outputs[0].reshape(NR, NA, NZ, D)
    grad_shifted = outputs[1].reshape(NR, NA, NZ, D)
    rows_back = jnp.arange(NR, dtype=jnp.int32) - shift_rad
    wrap_back = (rows_back < 0).astype(jnp.int32)
    rows_back = rows_back % NR
    cols_back = (jnp.arange(NA, dtype=jnp.int32)[None, :] - shift_azi - offset * wrap_back[:, None]) % NA
    levels_back = (jnp.arange(NZ, dtype=jnp.int32) - shift_ver) % NZ
    block_out = out_shifted[rows_back[:, None], cols_back][:, :, levels_back]
    grad_tokens = grad_shifted[rows_back[:, None], cols_back][:, :, levels_back]
    factor = float(TOKENS) ** (-0.5)
    return (block_out, grad_tokens, totals[0] * factor, totals[1] * factor, totals[2] * factor)
```

```python
import jax
import jax.numpy as jnp
from jax import lax
from jax.experimental import pallas as pl
from jax.experimental.pallas import tpu as pltpu
from jax.sharding import PartitionSpec as P

HEADS = 16
HD = 32
WR = 4
WA = 8
RIM = WR - 1
SIDE = WA // 2
EPS = 1e-05
F32 = jnp.float32
BF16 = jnp.bfloat16
NN = (((1,), (0,)), ((), ()))
NT = (((1,), (1,)), ((), ()))
TN = (((0,), (0,)), ((), ()))
TT = (((0,), (1,)), ((), ()))
LANES = 128
NX, NZ, NC = 2, 8, 2
FAR = (4, 3, 5, 2, 6, 1, 7)
UNROLL = 2
VMEM_LIMIT = 60 * 2 ** 20


def mm(a, b, dims=NN):
    return lax.dot_general(a, b, dims, preferred_element_type=F32)


class Wire:
    def __init__(self, send, recv):
        self.send, self.recv, self.used = send, recv, 0
        self.rad, self.azi = lax.axis_index("rad"), lax.axis_index("azi")
        self.waits = []

    def slot(self, count=1):
        first = self.used
        self.used += count
        return first

    def copy(self, src, dst, slot, rad=None, azi=None, recv_slot=None):
        rad = self.rad if rad is None else rad
        azi = self.azi if azi is None else azi
        return pltpu.make_async_remote_copy(
            src_ref=src,
            dst_ref=dst,
            send_sem=self.send.at[slot],
            recv_sem=self.recv.at[slot if recv_slot is None else recv_slot],
            device_id=(rad, azi),
            device_id_type=pl.DeviceIdType.MESH,
        )

    def local(self, src, dst, slot):
        return pltpu.make_async_copy(src, dst, self.recv.at[slot])


def greet(n_rad, n_azi):
    rad, azi = lax.axis_index("rad"), lax.axis_index("azi")
    barrier = pltpu.get_barrier_semaphore()
    for step in range(1, n_azi):
        pl.semaphore_signal(
            barrier, inc=1, device_id=(rad, (azi + step) % n_azi),
            device_id_type=pl.DeviceIdType.MESH)
    for step in range(1, n_rad):
        pl.semaphore_signal(
            barrier, inc=1, device_id=((rad + step) % n_rad, azi),
            device_id_type=pl.DeviceIdType.MESH)
    pl.semaphore_wait(barrier, n_azi + n_rad - 2)


def edges(wire, srcs, ext, par, cur, got, pair, stage, n_rad, n_azi, down):
    rad, azi = wire.rad, wire.azi
    rows = srcs[0].shape[0]
    cols = srcs[0].shape[1]
    start, finish = (0, n_rad - 1) if down else (n_rad - 1, 0)
    step_rad = -1 if down else 1
    rim = pl.ds(0, RIM) if down else pl.ds(rows - RIM, RIM)
    own = pl.ds(0, rows) if down else pl.ds(RIM, rows)
    far = pl.ds(rows, RIM) if down else pl.ds(0, RIM)
    middle = pl.ds(SIDE, cols)
    low, high = pl.ds(0, SIDE), pl.ds(cols + SIDE, SIDE)
    before, after = (azi + n_azi - 1) % n_azi, (azi + 1) % n_azi
    quarters = srcs[0].shape[3] // LANES

    def piece(g):
        return srcs[g // quarters].at[rim, :, :, pl.ds(g % quarters * LANES, LANES)]

    s_scatter = wire.slot(n_rad)
    scatter = [
        wire.copy(piece(g), cur.at[0], s_scatter + g, rad=g, recv_slot=s_scatter)
        for g in range(n_rad)
    ]
    scatter_own = wire.local(piece(start), cur.at[0], s_scatter)

    @pl.when(rad == start)
    def _():
        scatter_own.start()
        for g in range(n_rad):
            if g != start:
                scatter[g].start()

    s_rim = wire.slot(2)
    rims = [
        wire.copy(srcs[t].at[rim], ext.at[t, far, middle], s_rim + t,
                  rad=(rad + step_rad + n_rad) % n_rad)
        for t in range(2)
    ]

    @pl.when(rad != start)
    def _():
        for copy in rims:
            copy.start()

    s_side = wire.slot(4)
    sides = []
    for t in range(2):
        sides.append(wire.copy(srcs[t].at[:, pl.ds(0, SIDE)], ext.at[t, own, high],
                               s_side + 2 * t, azi=before))
        sides.append(wire.copy(srcs[t].at[:, pl.ds(cols - SIDE, SIDE)], ext.at[t, own, low],
                               s_side + 2 * t + 1, azi=after))
    for copy in sides:
        copy.start()
    s_local = wire.slot(2)
    locals_ = [wire.local(srcs[t], ext.at[t, own, middle], s_local + t) for t in range(2)]
    for copy in locals_:
        copy.start()
    yield

    @pl.when(rad == start)
    def _():
        scatter_own.wait()

    @pl.when(rad != start)
    def _():
        scatter[start].wait_recv()

    hops = []
    s_hop = wire.slot(6)
    bits = (4, 0, 1, 2, 3)
    for k, bit in enumerate(bits):
        hop = wire.copy(cur.at[k], got.at[k], s_hop + k,
                        azi=(azi + n_azi - (1 << bit)) % n_azi)
        hop.start()
        hops.append(hop)
        yield
        hop.wait_recv()
        chosen = par[1 + bit] == 1
        value = jnp.where(chosen, got[k], cur[k])
        if k + 1 < len(bits):
            cur[k + 1] = value
        else:
            pair[:, :cols] = value
    hop = wire.copy(pair.at[:, pl.ds(0, cols)], pair.at[:, pl.ds(cols, cols)], s_hop + 5,
                    azi=before)
    hop.start()
    hops.append(hop)
    yield
    hop.wait_recv()
    stage[...] = pair[:, pl.ds(par[0], cols)]
    s_last = wire.slot(n_rad)
    lanes = pl.ds(pl.multiple_of(rad % quarters * LANES, LANES), LANES)
    last = wire.copy(stage, ext.at[rad // quarters, far, pl.ds(0, cols), :, lanes],
                     s_last, rad=finish, recv_slot=s_last + rad)
    last_own = wire.local(stage, ext.at[rad // quarters, far, pl.ds(0, cols), :, lanes],
                          s_last + finish)

    @pl.when(rad == finish)
    def _():
        last_own.start()

    @pl.when(rad != finish)
    def _():
        last.start()

    yield
    s_corner = wire.slot(2)
    corners = [
        wire.copy(ext.at[:, far, pl.ds(SIDE, SIDE)], ext.at[:, far, high], s_corner, azi=before),
        wire.copy(ext.at[:, far, pl.ds(cols, SIDE)], ext.at[:, far, low], s_corner + 1, azi=after),
    ]

    @pl.when(rad != finish)
    def _():
        for copy in rims:
            copy.wait_recv()
        for copy in corners:
            copy.start()

    yield
    for copy in locals_:
        copy.wait()
    for copy in sides:
        copy.wait()
    for hop in hops:
        hop.wait_send()

    @pl.when(rad != finish)
    def _():
        for copy in corners:
            copy.wait()
        last.wait_send()

    @pl.when(rad == finish)
    def _():
        last_own.wait()
        for g in range(n_rad):
            if g != finish:
                wire.copy(stage, ext.at[g // quarters, far, pl.ds(0, cols), :,
                                        pl.ds(g % quarters * LANES, LANES)],
                          s_last, rad=finish, recv_slot=s_last + g).wait_recv()

    @pl.when(rad != start)
    def _():
        for copy in rims:
            copy.wait_send()

    @pl.when(rad == start)
    def _():
        for g in range(n_rad):
            if g != start:
                scatter[g].wait_send()


def place(azi):
    return azi // (NZ * NC), azi // NC % NZ, azi % NC


def index(x, z, c):
    return (x * NZ + z) * NC + c


def gather_weights(wire, w, w_all):
    azi = wire.azi
    x, z, c = place(azi)
    across, partner = index(1 - x, z, c), index(x, z, 1 - c)
    s_own, s_z, s_x, s_c = wire.slot(), wire.slot(NZ), wire.slot(NZ), wire.slot(2 * NZ)
    own = wire.local(w, w_all.at[azi], s_own)
    own.start()
    sent = []
    along = {}
    for k in FAR:
        along[k] = wire.copy(w, w_all.at[azi], s_z + k, azi=index(x, (z + k) % NZ, c))
        along[k].start()
    first = [
        wire.copy(w, w_all.at[azi], s_x, azi=across),
        wire.copy(w, w_all.at[azi], s_c, azi=partner),
    ]
    for copy in first:
        copy.start()
    yield
    near = (1, 7, 2, 6, 3, 5, 4)
    xs, cs = {0: first[0]}, {0: first[1]}
    for count, k in enumerate(near):
        came = index(x, (z + NZ - k) % NZ, c)
        wire.copy(w, w_all.at[came], s_z + k, azi=azi).wait_recv()
        xs[k] = wire.copy(w_all.at[came], w_all.at[came], s_x + k, azi=across)
        cs[k] = wire.copy(w_all.at[came], w_all.at[came], s_c + k, azi=partner)
        xs[k].start()
        cs[k].start()
        if count % 2 == 1:
            yield
    for count, k in enumerate((0,) + near):
        came = index(1 - x, (z + NZ - k) % NZ, c)
        wire.copy(w, w_all.at[came], s_x + k, azi=azi).wait_recv()
        cs[NZ + k] = wire.copy(w_all.at[came], w_all.at[came], s_c + NZ + k, azi=partner)
        cs[NZ + k].start()
        if count % 3 == 2:
            yield
    own.wait()
    for k in range(NZ):
        wire.copy(w, w_all.at[index(x, (z + NZ - k) % NZ, 1 - c)], s_c + k, azi=azi).wait_recv()
        wire.copy(w, w_all.at[index(1 - x, (z + NZ - k) % NZ, 1 - c)], s_c + NZ + k,
                  azi=azi).wait_recv()
    for k in range(NZ):
        if k:
            along[k].wait_send()
        xs[k].wait_send()
        cs[k].wait_send()
        cs[NZ + k].wait_send()


def sum_weights(wire, acc, gsum, share, gtot, r1, r2, s1, s2, r3, s3, r4, s4, gbuf, gz, gr,
                n_rad):
    rad, azi = wire.rad, wire.azi
    x, z, c = place(azi)
    across, partner = index(1 - x, z, c), index(x, z, 1 - c)
    s_c, s_x, s_z = wire.slot(2 * NZ), wire.slot(NZ), wire.slot(NZ)
    s_g = wire.slot(2)
    s_gz = wire.slot(NZ)
    order = FAR + (0,)
    core = {}
    for half in (1, 0):
        for k in order:
            xx = (x + half) % NX
            zz = (z + k) % NZ
            core[half, k] = wire.copy(acc.at[index(xx, zz, 1 - c)], r1.at[half, k],
                                      s_c + half * NZ + k, azi=partner)
            core[half, k].start()
    g_core = wire.copy(gsum, gbuf.at[0], s_g, azi=partner)
    g_core.start()
    yield
    xs, zs = {}, {}
    for k in order:
        core[1, k].wait_recv()
        mine = acc[index(1 - x, (z + k) % NZ, c)]
        s1[k] = (mine.astype(F32) + r1[1, k].astype(F32)).astype(BF16)
        xs[k] = wire.copy(s1.at[k], r2.at[k], s_x + k, azi=across)
        xs[k].start()
    g_core.wait_recv()
    gbuf[1] = gsum[...] + gbuf[0]
    g_x = wire.copy(gbuf.at[1], gbuf.at[2], s_g + 1, azi=across)
    g_x.start()
    yield
    for count, k in enumerate(order):
        core[0, k].wait_recv()
        xs[k].wait_recv()
        mine = acc[index(x, (z + k) % NZ, c)]
        total = mine.astype(F32) + r1[0, k].astype(F32) + r2[k].astype(F32)
        s2[k] = total.astype(BF16)
        if k:
            zs[k] = wire.copy(s2.at[k], r3.at[k], s_z + k, azi=index(x, (z + k) % NZ, c))
            zs[k].start()
        if count % 3 == 2:
            yield
    g_x.wait_recv()
    gz[z] = gbuf[1] + gbuf[2]
    g_zs = {}
    for k in FAR:
        g_zs[k] = wire.copy(gz.at[z], gz.at[z], s_gz + k, azi=index(x, (z + k) % NZ, c))
        g_zs[k].start()
    yield
    total = s2[0].astype(F32)
    for k in (1, 7, 2, 6, 3, 5, 4):
        zs[k].wait_recv()
        total = total + r3[k].astype(F32)
    part = s4.shape[1]
    for g in range(n_rad):
        s3[g] = total[:, part * g: part * (g + 1)].astype(BF16)
    s_r, s_a, s_gr = wire.slot(n_rad), wire.slot(n_rad), wire.slot(n_rad)
    outs = []
    for k in range(1, n_rad):
        to = (rad + k) % n_rad
        copy = wire.copy(s3.at[to], r4.at[k], s_r + k, rad=to)
        copy.start()
        outs.append(copy)
    for k in FAR:
        wire.copy(gz.at[z], gz.at[(z + NZ - k) % NZ], s_gz + k, azi=azi).wait_recv()
    value = gz[0]
    for k in range(1, NZ):
        value = value + gz[k]
    gr[rad] = value
    g_outs = []
    for k in range(1, n_rad):
        copy = wire.copy(gr.at[rad], gr.at[rad], s_gr + k, rad=(rad + k) % n_rad)
        copy.start()
        g_outs.append(copy)
    yield
    total = s3[rad].astype(F32)
    for k in range(1, n_rad):
        outs[k - 1].wait_recv()
        total = total + r4[k].astype(F32)
    s4[...] = total.astype(BF16)
    share[rad] = s4[...]
    finals = []
    for k in range(1, n_rad):
        copy = wire.copy(s4, share.at[rad], s_a + k, rad=(rad + k) % n_rad)
        copy.start()
        finals.append(copy)
    yield
    for k in range(1, n_rad):
        wire.copy(gr.at[rad], gr.at[(rad + n_rad - k) % n_rad], s_gr + k, rad=rad).wait_recv()
    value = gr[0]
    for k in range(1, n_rad):
        value = value + gr[k]
    gtot[...] = value
    for k in range(1, n_rad):
        wire.copy(s4, share.at[(rad + n_rad - k) % n_rad], s_a + k, rad=rad).wait_recv()
    for copy in list(core.values()) + list(xs.values()) + list(zs.values()) + list(g_zs.values()):
        copy.wait_send()
    for copy in outs + g_outs + finals + [g_core, g_x]:
        copy.wait_send()


def interleave(*runs):
    live = list(runs)
    while live:
        for run in list(live):
            try:
                next(run)
            except StopIteration:
                live.remove(run)


COPIES = 112


def collect_kernel(n_rad, n_azi, par, tok, cot, w, ext, w_all, cur, got, pair, stage, send, recv):
    greet(n_rad, n_azi)
    wire = Wire(send, recv)
    interleave(
        edges(wire, (tok, cot), ext, par, cur, got, pair, stage, n_rad, n_azi, True),
        gather_weights(wire, w, w_all),
    )


def deliver_kernel(n_rad, n_azi, par, frame, acc, gsum, ext, share, gtot, cur, got, pair, stage,
                   r1, r2, s1, s2, r3, s3, r4, s4, gbuf, gz, gr, send, recv):
    greet(n_rad, n_azi)
    wire = Wire(send, recv)
    interleave(
        edges(wire, (frame.at[0], frame.at[1]), ext, par, cur, got, pair, stage, n_rad, n_azi,
              False),
        sum_weights(wire, acc, gsum, share, gtot, r1, r2, s1, s2, r3, s3, r4, s4, gbuf, gz, gr,
                    n_rad),
    )


def roll_scratch(cols, depth):
    return [
        pltpu.VMEM((5, RIM, cols, depth, LANES), BF16),
        pltpu.VMEM((5, RIM, cols, depth, LANES), BF16),
        pltpu.VMEM((RIM, 2 * cols, depth, LANES), BF16),
        pltpu.VMEM((RIM, cols, depth, LANES), BF16),
    ]


def semaphores():
    return [pltpu.SemaphoreType.DMA((COPIES,)), pltpu.SemaphoreType.DMA((COPIES,))]


VM = pl.BlockSpec(memory_space=pltpu.VMEM)
SM = pl.BlockSpec(memory_space=pltpu.SMEM)
ANY = pl.BlockSpec(memory_space=pl.ANY)


def collect(par, tok, cot, w, n_rad, n_azi):
    rows, cols, depth, width = tok.shape

    def kernel(*refs):
        collect_kernel(n_rad, n_azi, *refs)

    return pl.pallas_call(
        kernel,
        out_shape=(
            jax.ShapeDtypeStruct((2, rows + RIM, cols + 2 * SIDE, depth, width), BF16),
            jax.ShapeDtypeStruct((n_azi,) + w.shape, BF16),
        ),
        in_specs=[SM, ANY, ANY, VM],
        out_specs=(VM, VM),
        scratch_shapes=roll_scratch(cols, depth) + semaphores(),
        compiler_params=pltpu.CompilerParams(
            collective_id=0, has_side_effects=True, vmem_limit_bytes=VMEM_LIMIT),
    )(par, tok, cot, w)


def deliver(par, frame, acc, gsum, n_rad, n_azi):
    _, rows, cols, depth, width = frame.shape
    _, deep, wide = acc.shape
    part = wide // n_rad

    def kernel(*refs):
        deliver_kernel(n_rad, n_azi, *refs)

    return pl.pallas_call(
        kernel,
        out_shape=(
            jax.ShapeDtypeStruct((2, rows + RIM, cols + 2 * SIDE, depth, width), BF16),
            jax.ShapeDtypeStruct((n_rad, deep, part), BF16),
            jax.ShapeDtypeStruct(gsum.shape, F32),
        ),
        in_specs=[SM, VM, VM, VM],
        out_specs=(VM, VM, VM),
        scratch_shapes=roll_scratch(cols, depth) + [
            pltpu.VMEM((NX, NZ, deep, wide), BF16),
            pltpu.VMEM((NZ, deep, wide), BF16),
            pltpu.VMEM((NZ, deep, wide), BF16),
            pltpu.VMEM((NZ, deep, wide), BF16),
            pltpu.VMEM((NZ, deep, wide), BF16),
            pltpu.VMEM((n_rad, deep, part), BF16),
            pltpu.VMEM((n_rad, deep, part), BF16),
            pltpu.VMEM((deep, part), BF16),
            pltpu.VMEM((3,) + gsum.shape, F32),
            pltpu.VMEM((NZ,) + gsum.shape, F32),
            pltpu.VMEM((n_rad,) + gsum.shape, F32),
        ] + semaphores(),
        compiler_params=pltpu.CompilerParams(
            collective_id=1, has_side_effects=True, vmem_limit_bytes=VMEM_LIMIT),
    )(par, frame, acc, gsum)


def block_kernel(par, ext_ref, gain_ref, w_ref, frame_ref, low_ref, gsum_ref,
                 acc_ref, qkv_t, dat_t, att_t, dqkv_t):
    i = pl.program_id(0)
    j = pl.program_id(1)
    width = gain_ref.shape[1]
    depth = ext_ref.shape[3]
    rows = frame_ref.shape[1]
    n = WR * WA * depth

    @pl.when((i == 0) & (j == 0))
    def _():
        acc_ref[...] = jnp.zeros_like(acc_ref)
        gsum_ref[...] = jnp.zeros_like(gsum_ref)

    def window(t):
        parts = []
        for r in range(WR):
            row = par[0] + WR * i + r
            first = jnp.where(row >= rows, par[2], par[1]) + WA * j
            parts.append(ext_ref[t, row, pl.ds(first, WA)].astype(F32).reshape(WA * depth, width))
        return jnp.concatenate(parts, axis=0)

    x = window(0)
    g = window(1)
    gain = gain_ref[...]
    wqkv = w_ref.at[:, pl.ds(0, 3 * width)]
    wout = w_ref.at[:, pl.ds(3 * width, width)]
    centred = x - jnp.mean(x, axis=1, keepdims=True)
    inv = lax.rsqrt(jnp.mean(centred * centred, axis=1, keepdims=True) + EPS)
    xhat = centred * inv
    hidden = (xhat * gain).astype(BF16)
    g_low = g.astype(BF16)
    qkv_t[...] = mm(hidden, wqkv[...]).T.astype(BF16)
    dat_t[...] = mm(g_low, wout[...], NT).T.astype(BF16)
    scale = HD ** -0.5

    def head(h, carry):
        at = pl.multiple_of(h * HD, HD)
        q = qkv_t[pl.ds(at, HD), :]
        k = qkv_t[pl.ds(width + at, HD), :]
        v = qkv_t[pl.ds(2 * width + at, HD), :]
        d = dat_t[pl.ds(at, HD), :]
        s = mm(k, q, TN)
        e = jnp.exp((s - jnp.max(s, axis=0, keepdims=True)) * scale)
        p = e * (1.0 / jnp.sum(e, axis=0, keepdims=True))
        low = p.astype(BF16)
        att = mm(v, low)
        att_t[pl.ds(at, HD), :] = att.astype(BF16)
        dp = mm(v, d, TN)
        dot = jnp.sum(att * d.astype(F32), axis=0, keepdims=True)
        ds = (p * (dp - dot)).astype(BF16)
        dqkv_t[pl.ds(at, HD), :] = (mm(k, ds) * scale).astype(BF16)
        dqkv_t[pl.ds(width + at, HD), :] = (mm(q, ds, NT) * scale).astype(BF16)
        dqkv_t[pl.ds(2 * width + at, HD), :] = mm(d, low, NT).astype(BF16)
        return carry

    lax.fori_loop(0, HEADS, head, 0, unroll=UNROLL)

    shape = (WR, WA, depth, width)
    own, cols = pl.ds(WR * i, WR), pl.ds(WA * j, WA)
    att_all = att_t[...]
    y = x + mm(att_all, wout[...], TN)
    frame_ref[0, own, cols] = y.reshape(shape).astype(BF16)
    dqkv = dqkv_t[...]
    acc_ref[:, : 3 * width] += mm(hidden, dqkv, TT)
    acc_ref[:, 3 * width:] += mm(att_all, g_low)
    dh = mm(dqkv, wqkv[...], TT)
    gsum_ref[...] += jnp.sum(dh * xhat, axis=0, keepdims=True)
    dx = dh * gain
    dx = inv * (dx - jnp.mean(dx, axis=1, keepdims=True)
                - xhat * jnp.mean(dx * xhat, axis=1, keepdims=True))
    frame_ref[1, own, cols] = (g + dx).reshape(shape).astype(BF16)

    @pl.when((i == pl.num_programs(0) - 1) & (j == pl.num_programs(1) - 1))
    def _():
        low_ref[...] = acc_ref[...].astype(BF16)


def block(par, ext, gain, w, rows, cols):
    width = gain.shape[1]
    depth = ext.shape[3]
    n = WR * WA * depth
    return pl.pallas_call(
        block_kernel,
        grid=(rows // WR, cols // WA),
        out_shape=(
            jax.ShapeDtypeStruct((2, rows, cols, depth, width), BF16),
            jax.ShapeDtypeStruct((width, 4 * width), BF16),
            jax.ShapeDtypeStruct((1, width), F32),
        ),
        in_specs=[SM, VM, VM, VM],
        out_specs=(VM, VM, VM),
        scratch_shapes=[
            pltpu.VMEM((width, 4 * width), F32),
            pltpu.VMEM((3 * width, n), BF16),
            pltpu.VMEM((width, n), BF16),
            pltpu.VMEM((width, n), BF16),
            pltpu.VMEM((3 * width, n), BF16),
        ],
        compiler_params=pltpu.CompilerParams(vmem_limit_bytes=VMEM_LIMIT),
    )(par, ext, gain, w)


def settle_kernel(par, ext_ref, out_ref, grad_ref):
    rows, cols = out_ref.shape[:2]
    for t, ref in enumerate((out_ref, grad_ref)):
        for r in range(rows):
            row = par[0] + r
            first = jnp.where(row < RIM, par[2], par[1])
            ref[r] = ext_ref[t, row, pl.ds(first, cols)]


def settle(par, ext, rows, cols):
    depth, width = ext.shape[3:]
    shape = jax.ShapeDtypeStruct((rows, cols, depth, width), BF16)
    return pl.pallas_call(
        settle_kernel,
        out_shape=(shape, shape),
        in_specs=[SM, VM],
        out_specs=(VM, VM),
        compiler_params=pltpu.CompilerParams(vmem_limit_bytes=VMEM_LIMIT),
    )(par, ext)


def roll_par(amount, cols):
    hops = amount // cols
    return jnp.stack([amount % cols] + [(hops >> bit) & 1 for bit in range(5)]).astype(jnp.int32)


def on_device(tokens, cotangent, ln_gain, qkv_weight, out_weight, shear_offset, window_shift):
    rows, cols, depth, width = tokens.shape
    n_rad, n_azi = lax.axis_size("rad"), lax.axis_size("azi")
    rad = lax.axis_index("rad")
    total = cols * n_azi
    shift_rad, shift_azi = window_shift[0], window_shift[1]
    lean = jnp.where(shift_azi > SIDE, shift_azi - WA, shift_azi)
    forth = (shear_offset[0] + lean + total) % total
    back = (total - forth) % total
    par_in = roll_par(forth, cols)
    par_out = roll_par(back, cols)
    inner, outer = SIDE + lean, SIDE - lean
    par_mid = jnp.stack([shift_rad, inner, jnp.where(rad == n_rad - 1, 0, inner)])
    par_end = jnp.stack([RIM - shift_rad, outer, jnp.where(rad == 0, 0, outer)])
    w = jnp.concatenate([qkv_weight, out_weight], axis=1)
    ext, w_all = collect(par_in, tokens, cotangent, w, n_rad, n_azi)
    frame, acc, gsum = block(par_mid.astype(jnp.int32), ext, ln_gain.reshape(1, width),
                             w_all.reshape(width, 4 * width), rows, cols)
    ext_out, share, gtot = deliver(par_out, frame, acc.reshape(n_azi, width // n_azi, 4 * width),
                                   gsum, n_rad, n_azi)
    block_out, grad_tokens = settle(par_end.astype(jnp.int32), ext_out, rows, cols)
    factor = float(rows * cols * depth * n_rad * n_azi) ** (-0.5)
    share = share.transpose(1, 0, 2).reshape(width // n_azi, 4 * width).astype(F32) * factor
    return (block_out, grad_tokens, share[:, : 3 * width], share[:, 3 * width:],
            gtot.reshape(width) * factor)


def solution(mesh):
    in_specs = (
        P("rad", "azi", None, None),
        P("rad", "azi", None, None),
        P(),
        P("azi", None),
        P("azi", None),
        P(),
        P(),
    )
    out_specs = (
        P("rad", "azi", None, None),
        P("rad", "azi", None, None),
        P("azi", None),
        P("azi", None),
        P(),
    )
    return jax.shard_map(
        on_device, mesh=mesh, in_specs=in_specs, out_specs=out_specs, check_vma=False
    )
```

```python
import jax
import jax.numpy as jnp
from jax import lax
from jax.experimental import pallas as pl
from jax.experimental.pallas import tpu as pltpu
from jax.sharding import PartitionSpec as P

HEADS = 16
HD = 32
WR = 4
WA = 8
RIM = WR - 1
SIDE = WA // 2
EPS = 1e-05
F32 = jnp.float32
BF16 = jnp.bfloat16
NN = (((1,), (0,)), ((), ()))
NT = (((1,), (1,)), ((), ()))
TN = (((0,), (0,)), ((), ()))
TT = (((0,), (1,)), ((), ()))
LANES = 128
NX, NZ, NC = 2, 8, 2
FAR = (4, 3, 5, 2, 6, 1, 7)
UNROLL = 2
VMEM_LIMIT = 60 * 2 ** 20


def mm(a, b, dims=NN):
    return lax.dot_general(a, b, dims, preferred_element_type=F32)


class Wire:
    def __init__(self, send, recv):
        self.send, self.recv, self.used = send, recv, 0
        self.rad, self.azi = lax.axis_index("rad"), lax.axis_index("azi")
        self.waits = []

    def slot(self, count=1):
        first = self.used
        self.used += count
        return first

    def copy(self, src, dst, slot, rad=None, azi=None, recv_slot=None):
        rad = self.rad if rad is None else rad
        azi = self.azi if azi is None else azi
        return pltpu.make_async_remote_copy(
            src_ref=src,
            dst_ref=dst,
            send_sem=self.send.at[slot],
            recv_sem=self.recv.at[slot if recv_slot is None else recv_slot],
            device_id=(rad, azi),
            device_id_type=pl.DeviceIdType.MESH,
        )

    def local(self, src, dst, slot):
        return pltpu.make_async_copy(src, dst, self.recv.at[slot])


def greet(n_rad, n_azi):
    rad, azi = lax.axis_index("rad"), lax.axis_index("azi")
    barrier = pltpu.get_barrier_semaphore()
    for step in range(1, n_azi):
        pl.semaphore_signal(
            barrier, inc=1, device_id=(rad, (azi + step) % n_azi),
            device_id_type=pl.DeviceIdType.MESH)
    for step in range(1, n_rad):
        pl.semaphore_signal(
            barrier, inc=1, device_id=((rad + step) % n_rad, azi),
            device_id_type=pl.DeviceIdType.MESH)
    pl.semaphore_wait(barrier, n_azi + n_rad - 2)


def roll(wire, take, piece_in, start, finish, bits, rem, land, cur, got, pair, stage, n_rad, n_azi):
    rad, azi = wire.rad, wire.azi
    cols = stage.shape[1]
    quarters = n_rad // 2
    s_scatter = wire.slot(n_rad)
    scatter = [
        wire.copy(take(g), cur.at[0], s_scatter + g, rad=g, recv_slot=s_scatter)
        for g in range(n_rad)
    ]
    scatter_own = wire.local(take(start), cur.at[0], s_scatter)

    @pl.when(rad == start)
    def _():
        for g in range(n_rad):
            if g != start:
                scatter[g].start()
        scatter_own.start()

    yield

    @pl.when(rad == start)
    def _():
        scatter_own.wait()

    @pl.when(rad != start)
    def _():
        scatter[start].wait_recv()

    hops = []
    s_hop = wire.slot(6)
    order = (4, 0, 1, 2, 3)
    for k, bit in enumerate(order):
        hop = wire.copy(cur.at[k], got.at[k], s_hop + k,
                        azi=(azi + n_azi - (1 << bit)) % n_azi)
        hop.start()
        hops.append(hop)
        yield
        hop.wait_recv()
        value = jnp.where(bits[bit] == 1, got[k], cur[k])
        if k + 1 < len(order):
            cur[k + 1] = value
        else:
            pair[:, :cols] = value
    hop = wire.copy(pair.at[:, pl.ds(0, cols)], pair.at[:, pl.ds(cols, cols)], s_hop + 5,
                    azi=(azi + n_azi - 1) % n_azi)
    hop.start()
    hops.append(hop)
    yield
    hop.wait_recv()
    stage[...] = pair[:, pl.ds(rem, cols)]
    s_last = wire.slot(n_rad)
    last = wire.copy(stage, land(rad // quarters, rad % quarters), s_last, rad=finish,
                     recv_slot=s_last + rad)
    last_own = wire.local(stage, land(finish // quarters, finish % quarters), s_last + finish)

    @pl.when(rad == finish)
    def _():
        last_own.start()

    @pl.when(rad != finish)
    def _():
        last.start()

    yield
    for hop in hops:
        hop.wait_send()

    @pl.when(rad != finish)
    def _():
        last.wait_send()

    @pl.when(rad == finish)
    def _():
        last_own.wait()
        for g in range(n_rad):
            if g != finish:
                wire.copy(stage, land(g // quarters, g % quarters), s_last, rad=finish,
                          recv_slot=s_last + g).wait_recv()

    @pl.when(rad == start)
    def _():
        for g in range(n_rad):
            if g != start:
                scatter[g].wait_send()


def rims(wire, take, far, start, finish, step_rad, cols, n_rad, n_azi):
    rad, azi = wire.rad, wire.azi
    before, after = (azi + n_azi - 1) % n_azi, (azi + 1) % n_azi
    middle = pl.ds(SIDE, cols)
    s_rim = wire.slot(2)
    moved = [
        wire.copy(take(t), far.at[t, :, middle], s_rim + t,
                  rad=(rad + step_rad + n_rad) % n_rad)
        for t in range(2)
    ]

    @pl.when(rad != start)
    def _():
        for copy in moved:
            copy.start()

    yield
    s_corner = wire.slot(2)
    corners = [
        wire.copy(far.at[:, :, pl.ds(SIDE, SIDE)], far.at[:, :, pl.ds(cols + SIDE, SIDE)],
                  s_corner, azi=before),
        wire.copy(far.at[:, :, pl.ds(cols, SIDE)], far.at[:, :, pl.ds(0, SIDE)],
                  s_corner + 1, azi=after),
    ]

    @pl.when(rad != finish)
    def _():
        for copy in moved:
            copy.wait_recv()
        for copy in corners:
            copy.start()

    yield

    @pl.when(rad != finish)
    def _():
        for copy in corners:
            copy.wait()

    @pl.when(rad != start)
    def _():
        for copy in moved:
            copy.wait_send()


def lane_block(f):
    return pl.ds(pl.multiple_of(f * LANES, LANES), LANES)


def place(azi):
    return azi // (NZ * NC), azi // NC % NZ, azi % NC


def index(x, z, c):
    return (x * NZ + z) * NC + c


def gather_weights(wire, w, w_all):
    azi = wire.azi
    x, z, c = place(azi)
    across, partner = index(1 - x, z, c), index(x, z, 1 - c)
    s_own, s_z, s_x, s_c = wire.slot(), wire.slot(NZ), wire.slot(NZ), wire.slot(2 * NZ)
    own = wire.local(w, w_all.at[azi], s_own)
    own.start()
    sent = []
    along = {}
    for k in FAR:
        along[k] = wire.copy(w, w_all.at[azi], s_z + k, azi=index(x, (z + k) % NZ, c))
        along[k].start()
    first = [
        wire.copy(w, w_all.at[azi], s_x, azi=across),
        wire.copy(w, w_all.at[azi], s_c, azi=partner),
    ]
    for copy in first:
        copy.start()
    yield
    near = (1, 7, 2, 6, 3, 5, 4)
    xs, cs = {0: first[0]}, {0: first[1]}
    for count, k in enumerate(near):
        came = index(x, (z + NZ - k) % NZ, c)
        wire.copy(w, w_all.at[came], s_z + k, azi=azi).wait_recv()
        xs[k] = wire.copy(w_all.at[came], w_all.at[came], s_x + k, azi=across)
        cs[k] = wire.copy(w_all.at[came], w_all.at[came], s_c + k, azi=partner)
        xs[k].start()
        cs[k].start()
        if count % 2 == 1:
            yield
    for count, k in enumerate((0,) + near):
        came = index(1 - x, (z + NZ - k) % NZ, c)
        wire.copy(w, w_all.at[came], s_x + k, azi=azi).wait_recv()
        cs[NZ + k] = wire.copy(w_all.at[came], w_all.at[came], s_c + NZ + k, azi=partner)
        cs[NZ + k].start()
        if count % 3 == 2:
            yield
    own.wait()
    for k in range(NZ):
        wire.copy(w, w_all.at[index(x, (z + NZ - k) % NZ, 1 - c)], s_c + k, azi=azi).wait_recv()
        wire.copy(w, w_all.at[index(1 - x, (z + NZ - k) % NZ, 1 - c)], s_c + NZ + k,
                  azi=azi).wait_recv()
    for k in range(NZ):
        if k:
            along[k].wait_send()
        xs[k].wait_send()
        cs[k].wait_send()
        cs[NZ + k].wait_send()


def block_of(acc, at, deep):
    return acc[pl.ds(pl.multiple_of(at * deep, deep), deep), :]


def sum_weights(wire, acc, low, gsum, share, gtot, r1, r2, s1, s2, r3, s3, r4, s4, gbuf, gz, gr,
                n_rad):
    rad, azi = wire.rad, wire.azi
    x, z, c = place(azi)
    across, partner = index(1 - x, z, c), index(x, z, 1 - c)
    s_c, s_x, s_z = wire.slot(2 * NZ), wire.slot(NZ), wire.slot(NZ)
    s_g = wire.slot(2)
    s_gz = wire.slot(NZ)
    order = FAR + (0,)
    deep = s4.shape[0]
    core = {}
    for half in (1, 0):
        for k in order:
            xx = (x + half) % NX
            zz = (z + k) % NZ
            low[half, k] = block_of(acc, index(xx, zz, 1 - c), deep).astype(BF16)
            core[half, k] = wire.copy(low.at[half, k], r1.at[half, k],
                                      s_c + half * NZ + k, azi=partner)
            core[half, k].start()
    g_core = wire.copy(gsum, gbuf.at[0], s_g, azi=partner)
    g_core.start()
    yield
    xs, zs = {}, {}
    for k in order:
        core[1, k].wait_recv()
        mine = block_of(acc, index(1 - x, (z + k) % NZ, c), deep)
        s1[k] = (mine + r1[1, k].astype(F32)).astype(BF16)
        xs[k] = wire.copy(s1.at[k], r2.at[k], s_x + k, azi=across)
        xs[k].start()
    g_core.wait_recv()
    gbuf[1] = gsum[...] + gbuf[0]
    g_x = wire.copy(gbuf.at[1], gbuf.at[2], s_g + 1, azi=across)
    g_x.start()
    yield
    for count, k in enumerate(order):
        core[0, k].wait_recv()
        xs[k].wait_recv()
        mine = block_of(acc, index(x, (z + k) % NZ, c), deep)
        total = mine + r1[0, k].astype(F32) + r2[k].astype(F32)
        s2[k] = total.astype(BF16)
        if k:
            zs[k] = wire.copy(s2.at[k], r3.at[k], s_z + k, azi=index(x, (z + k) % NZ, c))
            zs[k].start()
        if count % 3 == 2:
            yield
    g_x.wait_recv()
    gz[z] = gbuf[1] + gbuf[2]
    g_zs = {}
    for k in FAR:
        g_zs[k] = wire.copy(gz.at[z], gz.at[z], s_gz + k, azi=index(x, (z + k) % NZ, c))
        g_zs[k].start()
    yield
    total = s2[0].astype(F32)
    for k in (1, 7, 2, 6, 3, 5, 4):
        zs[k].wait_recv()
        total = total + r3[k].astype(F32)
    part = s4.shape[1]
    for g in range(n_rad):
        s3[g] = total[:, part * g: part * (g + 1)].astype(BF16)
    s_r, s_a, s_gr = wire.slot(n_rad), wire.slot(n_rad), wire.slot(n_rad)
    outs = []
    for k in range(1, n_rad):
        to = (rad + k) % n_rad
        copy = wire.copy(s3.at[to], r4.at[k], s_r + k, rad=to)
        copy.start()
        outs.append(copy)
    for k in FAR:
        wire.copy(gz.at[z], gz.at[(z + NZ - k) % NZ], s_gz + k, azi=azi).wait_recv()
    value = gz[0]
    for k in range(1, NZ):
        value = value + gz[k]
    gr[rad] = value
    g_outs = []
    for k in range(1, n_rad):
        copy = wire.copy(gr.at[rad], gr.at[rad], s_gr + k, rad=(rad + k) % n_rad)
        copy.start()
        g_outs.append(copy)
    yield
    total = s3[rad].astype(F32)
    for k in range(1, n_rad):
        outs[k - 1].wait_recv()
        total = total + r4[k].astype(F32)
    s4[...] = total.astype(BF16)
    share[rad] = s4[...]
    finals = []
    for k in range(1, n_rad):
        copy = wire.copy(s4, share.at[rad], s_a + k, rad=(rad + k) % n_rad)
        copy.start()
        finals.append(copy)
    yield
    for k in range(1, n_rad):
        wire.copy(gr.at[rad], gr.at[(rad + n_rad - k) % n_rad], s_gr + k, rad=rad).wait_recv()
    value = gr[0]
    for k in range(1, n_rad):
        value = value + gr[k]
    gtot[...] = value
    for k in range(1, n_rad):
        wire.copy(s4, share.at[(rad + n_rad - k) % n_rad], s_a + k, rad=rad).wait_recv()
    for copy in list(core.values()) + list(xs.values()) + list(zs.values()) + list(g_zs.values()):
        copy.wait_send()
    for copy in outs + g_outs + finals + [g_core, g_x]:
        copy.wait_send()


class Runs:
    def __init__(self):
        self.live = []

    def add(self, run):
        next(run)
        self.live.append(run)
        return run

    def tick(self):
        for run in list(self.live):
            if next(run, self) is self:
                self.live.remove(run)

    def finish(self, *runs):
        while any(run in self.live for run in (runs or self.live)):
            self.tick()


COPIES = 192
GROUPS = 4
VM = pl.BlockSpec(memory_space=pltpu.VMEM)
SM = pl.BlockSpec(memory_space=pltpu.SMEM)
ANY = pl.BlockSpec(memory_space=pl.ANY)


def layer_kernel(n_rad, n_azi, shear, shift, tok, cot, gain_ref, wqkv_own, wout_own,
                 ext, share, gtot,
                 main, far, w_own, w_all, cur, got, pair, stage, cur_b, got_b, pair_b, stage_b,
                 frame, acc, gsum, qkv_t, dat_t, att_t, dqkv_t,
                 low, r1, r2, s1, s2, r3, s3, r4, s4, gbuf, gz, gr, send, recv):
    wire = Wire(send, recv)
    rad, azi = wire.rad, wire.azi
    rows, cols, depth, width = tok.shape
    srcs = (tok, cot)
    n = WR * WA * depth
    before, after = (azi + n_azi - 1) % n_azi, (azi + 1) % n_azi
    middle, left, right = pl.ds(SIDE, cols), pl.ds(0, SIDE), pl.ds(cols + SIDE, SIDE)
    s_local = wire.slot(4)
    here = [
        wire.local(wqkv_own, w_own.at[:, pl.ds(0, 3 * width)], s_local),
        wire.local(wout_own, w_own.at[:, pl.ds(3 * width, width)], s_local + 1),
        wire.local(tok, main.at[0, :, middle], s_local + 2),
        wire.local(cot, main.at[1, :, middle], s_local + 3),
    ]
    for copy in here:
        copy.start()
    shift_rad, shift_azi = shift[0], shift[1]
    total_cols = cols * n_azi
    lean = jnp.where(shift_azi > SIDE, shift_azi - WA, shift_azi)
    forth = lax.rem(shear[0] + lean + total_cols, jnp.int32(total_cols))
    back = lax.rem(total_cols - forth, jnp.int32(total_cols))

    def parts(amount):
        hops = amount // cols
        return [(hops >> bit) & 1 for bit in range(5)], amount - hops * cols

    bits_in, rem_in = parts(forth)
    bits_out, rem_out = parts(back)
    acc[...] = jnp.zeros_like(acc)
    gsum[...] = jnp.zeros_like(gsum)
    greet(n_rad, n_azi)
    for copy in here[:2]:
        copy.wait()

    runs = Runs()
    weights = runs.add(gather_weights(wire, w_own, w_all.at[...]))
    s_side = wire.slot(4)
    sides = []
    for t in range(2):
        sides.append(wire.copy(srcs[t].at[:, pl.ds(0, SIDE)], main.at[t, :, right],
                               s_side + 2 * t, azi=before))
        sides.append(wire.copy(srcs[t].at[:, pl.ds(cols - SIDE, SIDE)], main.at[t, :, left],
                               s_side + 2 * t + 1, azi=after))
    for copy in sides:
        copy.start()
    quarters = n_rad // 2
    come = [
        runs.add(roll(
            wire,
            lambda g: srcs[g // quarters].at[pl.ds(0, RIM), :, :, lane_block(g % quarters)],
            None, 0, n_rad - 1, bits_in, rem_in,
            lambda t, f: far.at[t, :, pl.ds(0, cols), :, lane_block(f)],
            cur, got, pair, stage, n_rad, n_azi)),
        runs.add(rims(wire, lambda t: srcs[t].at[pl.ds(0, RIM)], far, 0, n_rad - 1, -1, cols,
                      n_rad, n_azi)),
    ]
    runs.finish(weights)
    for copy in here[2:]:
        copy.wait()
    for copy in sides:
        copy.wait()

    gain = gain_ref[...]
    deep = w_own.shape[0]
    wqkv = w_all.reshape(n_azi * deep, 4 * width).at[:, pl.ds(0, 3 * width)]
    wout = w_all.reshape(n_azi * deep, 4 * width).at[:, pl.ds(3 * width, width)]
    scale = HD ** -0.5
    col_near = SIDE + lean
    col_far = jnp.where(rad == n_rad - 1, 0, col_near)

    def line(t, i, j, r):
        row = shift_rad + WR * i + r
        near = main[t, jnp.minimum(row, rows - 1), pl.ds(col_near + WA * j, WA)].astype(F32)
        if WR * i + r + RIM < rows:
            return near
        other = far[t, jnp.maximum(row - rows, 0), pl.ds(col_far + WA * j, WA)].astype(F32)
        if WR * i + r + 1 >= rows:
            return other
        return jnp.where(row < rows, near, other)

    def window(i, j):
        def load(t):
            return jnp.concatenate(
                [line(t, i, j, r).reshape(WA * depth, width) for r in range(WR)], axis=0)

        x = load(0)
        g = load(1)
        centred = x - jnp.mean(x, axis=1, keepdims=True)
        inv = lax.rsqrt(jnp.mean(centred * centred, axis=1, keepdims=True) + EPS)
        xhat = centred * inv
        hidden = (xhat * gain).astype(BF16)
        g_low = g.astype(BF16)
        qkv_t[...] = mm(hidden, wqkv[...]).T.astype(BF16)
        dat_t[...] = mm(g_low, wout[...], NT).T.astype(BF16)

        def head(h, carry):
            at = pl.multiple_of(h * HD, HD)
            q = qkv_t[pl.ds(at, HD), :]
            k = qkv_t[pl.ds(width + at, HD), :]
            v = qkv_t[pl.ds(2 * width + at, HD), :]
            d = dat_t[pl.ds(at, HD), :]
            s = mm(k, q, TN)
            e = jnp.exp((s - jnp.max(s, axis=0, keepdims=True)) * scale)
            p = e * (1.0 / jnp.sum(e, axis=0, keepdims=True))
            low_p = p.astype(BF16)
            att = mm(v, low_p)
            att_t[pl.ds(at, HD), :] = att.astype(BF16)
            dp = mm(v, d, TN)
            dot = jnp.sum(att * d.astype(F32), axis=0, keepdims=True)
            ds = (p * (dp - dot)).astype(BF16)
            dqkv_t[pl.ds(at, HD), :] = (mm(k, ds) * scale).astype(BF16)
            dqkv_t[pl.ds(width + at, HD), :] = (mm(q, ds, NT) * scale).astype(BF16)
            dqkv_t[pl.ds(2 * width + at, HD), :] = mm(d, low_p, NT).astype(BF16)
            return carry

        each = HEADS // GROUPS
        for group in range(GROUPS):
            lax.fori_loop(group * each, (group + 1) * each, head, 0, unroll=UNROLL)
            runs.tick()
        shape = (WR, WA, depth, width)
        own, at = pl.ds(WR * i, WR), pl.ds(WA * j, WA)
        att_all = att_t[...]
        frame[0, own, at] = (x + mm(att_all, wout[...], TN)).reshape(shape).astype(BF16)
        dqkv = dqkv_t[...]
        acc[:, : 3 * width] += mm(hidden, dqkv, TT)
        acc[:, 3 * width:] += mm(att_all, g_low)
        dh = mm(dqkv, wqkv[...], TT)
        gsum[...] += jnp.sum(dh * xhat, axis=0, keepdims=True)
        dx = dh * gain
        dx = inv * (dx - jnp.mean(dx, axis=1, keepdims=True)
                    - xhat * jnp.mean(dx * xhat, axis=1, keepdims=True))
        frame[1, own, at] = (g + dx).reshape(shape).astype(BF16)

    s_out = wire.slot(8)
    back_sides = {}
    for i in range(2):
        own = pl.ds(WR * i, WR)
        there = pl.ds(RIM + WR * i, WR)
        back_sides[i, 0] = wire.copy(frame.at[:, own, pl.ds(0, SIDE)], ext.at[:, there, right],
                                     s_out + 2 * i, azi=before)
        back_sides[i, 1] = wire.copy(frame.at[:, own, pl.ds(cols - SIDE, SIDE)],
                                     ext.at[:, there, left], s_out + 2 * i + 1, azi=after)
    window(0, 0)
    back_sides[0, 0].start()
    runs.finish(*come)
    window(1, 0)
    window(1, 1)
    go = [
        runs.add(roll(
            wire,
            lambda g: frame.at[g // quarters, pl.ds(rows - RIM, RIM), :, :,
                               lane_block(g % quarters)],
            None, n_rad - 1, 0, bits_out, rem_out,
            lambda t, f: ext.at[t, pl.ds(0, RIM), pl.ds(0, cols), :, lane_block(f)],
            cur_b, got_b, pair_b, stage_b, n_rad, n_azi)),
        runs.add(rims(wire, lambda t: frame.at[t, pl.ds(rows - RIM, RIM)],
                      ext.at[:, pl.ds(0, RIM)], n_rad - 1, 0, 1, cols, n_rad, n_azi)),
    ]
    back_sides[1, 0].start()
    back_sides[1, 1].start()
    window(0, 1)
    back_sides[0, 1].start()
    final = [wire.local(frame.at[t], ext.at[t, pl.ds(RIM, rows), middle], s_out + 4 + t)
             for t in range(2)]
    for copy in final:
        copy.start()
    runs.add(sum_weights(wire, acc, low, gsum, share, gtot, r1, r2, s1, s2, r3, s3, r4, s4, gbuf,
                         gz, gr, n_rad))
    runs.finish()
    for copy in list(back_sides.values()) + final:
        copy.wait()


def layer(shear, shift, tok, cot, gain, wqkv, wout, n_rad, n_azi):
    rows, cols, depth, width = tok.shape
    deep, wide = wout.shape[0], 4 * width
    part = wide // n_rad
    n = WR * WA * depth
    across = cols + 2 * SIDE

    def kernel(*refs):
        layer_kernel(n_rad, n_azi, *refs)

    rolls = [
        pltpu.VMEM((5, RIM, cols, depth, LANES), BF16),
        pltpu.VMEM((5, RIM, cols, depth, LANES), BF16),
        pltpu.VMEM((RIM, 2 * cols, depth, LANES), BF16),
        pltpu.VMEM((RIM, cols, depth, LANES), BF16),
    ]
    return pl.pallas_call(
        kernel,
        out_shape=(
            jax.ShapeDtypeStruct((2, rows + RIM, across, depth, width), BF16),
            jax.ShapeDtypeStruct((n_rad, deep, part), BF16),
            jax.ShapeDtypeStruct((1, width), F32),
        ),
        in_specs=[SM, SM, ANY, ANY, VM, ANY, ANY],
        out_specs=(VM, VM, VM),
        scratch_shapes=[
            pltpu.VMEM((2, rows, across, depth, width), BF16),
            pltpu.VMEM((2, RIM, across, depth, width), BF16),
            pltpu.VMEM((deep, wide), BF16),
            pltpu.VMEM((n_azi, deep, wide), BF16),
        ] + rolls + rolls + [
            pltpu.VMEM((2, rows, cols, depth, width), BF16),
            pltpu.VMEM((width, wide), F32),
            pltpu.VMEM((1, width), F32),
            pltpu.VMEM((3 * width, n), BF16),
            pltpu.VMEM((width, n), BF16),
            pltpu.VMEM((width, n), BF16),
            pltpu.VMEM((3 * width, n), BF16),
            pltpu.VMEM((NX, NZ, deep, wide), BF16),
            pltpu.VMEM((NX, NZ, deep, wide), BF16),
            pltpu.VMEM((NZ, deep, wide), BF16),
            pltpu.VMEM((NZ, deep, wide), BF16),
            pltpu.VMEM((NZ, deep, wide), BF16),
            pltpu.VMEM((NZ, deep, wide), BF16),
            pltpu.VMEM((n_rad, deep, part), BF16),
            pltpu.VMEM((n_rad, deep, part), BF16),
            pltpu.VMEM((deep, part), BF16),
            pltpu.VMEM((3, 1, width), F32),
            pltpu.VMEM((NZ, 1, width), F32),
            pltpu.VMEM((n_rad, 1, width), F32),
            pltpu.SemaphoreType.DMA((COPIES,)),
            pltpu.SemaphoreType.DMA((COPIES,)),
        ],
        compiler_params=pltpu.CompilerParams(
            collective_id=0, has_side_effects=True, vmem_limit_bytes=VMEM_LIMIT),
    )(shear, shift, tok, cot, gain, wqkv, wout)


def settle_kernel(n_rad, shift, ext_ref, out_ref, grad_ref):
    rows, cols = out_ref.shape[:2]
    lean = jnp.where(shift[1] > SIDE, shift[1] - WA, shift[1])
    outer = SIDE - lean
    above = jnp.where(lax.axis_index("rad") == 0, 0, outer)
    for t, ref in enumerate((out_ref, grad_ref)):
        for r in range(rows):
            row = RIM - shift[0] + r
            first = jnp.where(row < RIM, above, outer)
            ref[r] = ext_ref[t, row, pl.ds(first, cols)]


def settle(shift, ext, rows, cols, n_rad):
    depth, width = ext.shape[3:]
    shape = jax.ShapeDtypeStruct((rows, cols, depth, width), BF16)

    def kernel(*refs):
        settle_kernel(n_rad, *refs)

    return pl.pallas_call(
        kernel,
        out_shape=(shape, shape),
        in_specs=[SM, VM],
        out_specs=(VM, VM),
        compiler_params=pltpu.CompilerParams(vmem_limit_bytes=VMEM_LIMIT),
    )(shift, ext)


def on_device(tokens, cotangent, ln_gain, qkv_weight, out_weight, shear_offset, window_shift):
    rows, cols, depth, width = tokens.shape
    n_rad, n_azi = lax.axis_size("rad"), lax.axis_size("azi")
    ext, share, gtot = layer(shear_offset, window_shift, tokens, cotangent,
                             ln_gain.reshape(1, width), qkv_weight, out_weight, n_rad, n_azi)
    block_out, grad_tokens = settle(window_shift, ext, rows, cols, n_rad)
    factor = float(rows * cols * depth * n_rad * n_azi) ** (-0.5)
    share = share.transpose(1, 0, 2).reshape(width // n_azi, 4 * width).astype(F32) * factor
    return (block_out, grad_tokens, share[:, : 3 * width], share[:, 3 * width:],
            gtot.reshape(width) * factor)


def solution(mesh):
    in_specs = (
        P("rad", "azi", None, None),
        P("rad", "azi", None, None),
        P(),
        P("azi", None),
        P("azi", None),
        P(),
        P(),
    )
    out_specs = (
        P("rad", "azi", None, None),
        P("rad", "azi", None, None),
        P("azi", None),
        P("azi", None),
        P(),
    )
    return jax.shard_map(
        on_device, mesh=mesh, in_specs=in_specs, out_specs=out_specs, check_vma=False
    )
```

```python
import jax
import jax.numpy as jnp
from jax import lax
from jax.experimental import pallas as pl
from jax.experimental.pallas import tpu as pltpu
from jax.sharding import PartitionSpec as P

HEADS = 16
HD = 32
WR = 4
WA = 8
RIM = WR - 1
SIDE = WA // 2
EPS = 1e-05
F32 = jnp.float32
BF16 = jnp.bfloat16
NN = (((1,), (0,)), ((), ()))
NT = (((1,), (1,)), ((), ()))
TN = (((0,), (0,)), ((), ()))
TT = (((0,), (1,)), ((), ()))
LANES = 128
NX, NZ, NC = 2, 8, 2
FAR = (4, 3, 5, 2, 6, 1, 7)
UNROLL = 2
VMEM_LIMIT = 60 * 2 ** 20


def mm(a, b, dims=NN):
    return lax.dot_general(a, b, dims, preferred_element_type=F32)


class Wire:
    def __init__(self, send, recv):
        self.send, self.recv, self.used = send, recv, 0
        self.rad, self.azi = lax.axis_index("rad"), lax.axis_index("azi")
        self.waits = []

    def slot(self, count=1):
        first = self.used
        self.used += count
        return first

    def copy(self, src, dst, slot, rad=None, azi=None, recv_slot=None):
        rad = self.rad if rad is None else rad
        azi = self.azi if azi is None else azi
        return pltpu.make_async_remote_copy(
            src_ref=src,
            dst_ref=dst,
            send_sem=self.send.at[slot],
            recv_sem=self.recv.at[slot if recv_slot is None else recv_slot],
            device_id=(rad, azi),
            device_id_type=pl.DeviceIdType.MESH,
        )

    def local(self, src, dst, slot):
        return pltpu.make_async_copy(src, dst, self.recv.at[slot])


def greet(n_rad, n_azi):
    rad, azi = lax.axis_index("rad"), lax.axis_index("azi")
    barrier = pltpu.get_barrier_semaphore()
    for step in range(1, n_azi):
        pl.semaphore_signal(
            barrier, inc=1, device_id=(rad, (azi + step) % n_azi),
            device_id_type=pl.DeviceIdType.MESH)
    for step in range(1, n_rad):
        pl.semaphore_signal(
            barrier, inc=1, device_id=((rad + step) % n_rad, azi),
            device_id_type=pl.DeviceIdType.MESH)
    pl.semaphore_wait(barrier, n_azi + n_rad - 2)


def roll(wire, take, start, finish, amount, land, cur, got, five, stage, n_rad, n_azi):
    rad, azi = wire.rad, wire.azi
    cols = stage.shape[1]
    quarters = n_rad // 2
    coarse = (amount + 2 * cols) // (4 * cols)
    rem = amount + 2 * cols - 4 * cols * coarse
    coarse = coarse & 7
    s_scatter = wire.slot(n_rad)
    scatter = [
        wire.copy(take(g), cur.at[0], s_scatter + g, rad=g, recv_slot=s_scatter)
        for g in range(n_rad)
    ]
    scatter_own = wire.local(take(start), cur.at[0], s_scatter)

    @pl.when(rad == start)
    def _():
        for g in range(n_rad):
            if g != start:
                scatter[g].start()
        scatter_own.start()

    yield

    @pl.when(rad == start)
    def _():
        scatter_own.wait()

    @pl.when(rad != start)
    def _():
        scatter[start].wait_recv()

    s_hop = wire.slot(8)

    def hop(src, dst, number, distance):
        copy = wire.copy(src, dst, s_hop + number, azi=(azi + n_azi - distance) % n_azi)
        copy.start()
        return copy

    hops = [hop(cur.at[0], got.at[0], 0, n_azi // 2)]
    yield
    hops[0].wait_recv()
    cur[1] = jnp.where(coarse >= 4, got[0], cur[0])
    for k in (2, 1, 3):
        hops.append(hop(cur.at[1], got.at[k], k, 4 * k))
    yield
    for copy in hops[1:]:
        copy.wait_recv()
    fine = coarse & 3
    near = jnp.where(fine == 1, got[1], cur[1])
    other = jnp.where(fine == 2, got[2], got[3])
    five[:, pl.ds(2 * cols, cols)] = jnp.where(fine >= 2, other, near)
    for number, k in enumerate((2, -2, 1, -1)):
        hops.append(hop(five.at[:, pl.ds(2 * cols, cols)],
                        five.at[:, pl.ds((2 + k) * cols, cols)], 4 + number, k))
    yield
    for copy in hops[4:]:
        copy.wait_recv()
    stage[...] = five[:, pl.ds(rem, cols)]
    s_last = wire.slot(n_rad)
    last = wire.copy(stage, land(rad // quarters, rad % quarters), s_last, rad=finish,
                     recv_slot=s_last + rad)
    last_own = wire.local(stage, land(finish // quarters, finish % quarters), s_last + finish)

    @pl.when(rad == finish)
    def _():
        last_own.start()

    @pl.when(rad != finish)
    def _():
        last.start()

    yield
    for copy in hops:
        copy.wait_send()

    @pl.when(rad != finish)
    def _():
        last.wait_send()

    @pl.when(rad == finish)
    def _():
        last_own.wait()
        for g in range(n_rad):
            if g != finish:
                wire.copy(stage, land(g // quarters, g % quarters), s_last, rad=finish,
                          recv_slot=s_last + g).wait_recv()

    @pl.when(rad == start)
    def _():
        for g in range(n_rad):
            if g != start:
                scatter[g].wait_send()


def rims(wire, take, far, start, finish, step_rad, cols, n_rad, n_azi):
    rad, azi = wire.rad, wire.azi
    before, after = (azi + n_azi - 1) % n_azi, (azi + 1) % n_azi
    middle = pl.ds(SIDE, cols)
    s_rim = wire.slot(2)
    moved = [
        wire.copy(take(t), far.at[t, :, middle], s_rim + t,
                  rad=(rad + step_rad + n_rad) % n_rad)
        for t in range(2)
    ]

    @pl.when(rad != start)
    def _():
        for copy in moved:
            copy.start()

    yield
    s_corner = wire.slot(2)
    corners = [
        wire.copy(far.at[:, :, pl.ds(SIDE, SIDE)], far.at[:, :, pl.ds(cols + SIDE, SIDE)],
                  s_corner, azi=before),
        wire.copy(far.at[:, :, pl.ds(cols, SIDE)], far.at[:, :, pl.ds(0, SIDE)],
                  s_corner + 1, azi=after),
    ]

    @pl.when(rad != finish)
    def _():
        for copy in moved:
            copy.wait_recv()
        for copy in corners:
            copy.start()

    yield

    @pl.when(rad != finish)
    def _():
        for copy in corners:
            copy.wait()

    @pl.when(rad != start)
    def _():
        for copy in moved:
            copy.wait_send()


def lane_block(f):
    return pl.ds(pl.multiple_of(f * LANES, LANES), LANES)


def place(azi):
    return azi // (NZ * NC), azi // NC % NZ, azi % NC


def index(x, z, c):
    return (x * NZ + z) * NC + c


def gather_weights(wire, w, w_all):
    azi = wire.azi
    x, z, c = place(azi)
    across, partner = index(1 - x, z, c), index(x, z, 1 - c)
    s_own, s_z, s_x, s_c = wire.slot(), wire.slot(NZ), wire.slot(NZ), wire.slot(2 * NZ)
    own = wire.local(w, w_all.at[azi], s_own)
    own.start()
    sent = []
    along = {}
    for k in FAR:
        along[k] = wire.copy(w, w_all.at[azi], s_z + k, azi=index(x, (z + k) % NZ, c))
        along[k].start()
    first = [
        wire.copy(w, w_all.at[azi], s_x, azi=across),
        wire.copy(w, w_all.at[azi], s_c, azi=partner),
    ]
    for copy in first:
        copy.start()
    yield
    near = (1, 7, 2, 6, 3, 5, 4)
    xs, cs = {0: first[0]}, {0: first[1]}
    for count, k in enumerate(near):
        came = index(x, (z + NZ - k) % NZ, c)
        wire.copy(w, w_all.at[came], s_z + k, azi=azi).wait_recv()
        xs[k] = wire.copy(w_all.at[came], w_all.at[came], s_x + k, azi=across)
        cs[k] = wire.copy(w_all.at[came], w_all.at[came], s_c + k, azi=partner)
        xs[k].start()
        cs[k].start()
        if count % 2 == 1:
            yield
    for count, k in enumerate((0,) + near):
        came = index(1 - x, (z + NZ - k) % NZ, c)
        wire.copy(w, w_all.at[came], s_x + k, azi=azi).wait_recv()
        cs[NZ + k] = wire.copy(w_all.at[came], w_all.at[came], s_c + NZ + k, azi=partner)
        cs[NZ + k].start()
        if count % 3 == 2:
            yield
    own.wait()
    for k in range(NZ):
        wire.copy(w, w_all.at[index(x, (z + NZ - k) % NZ, 1 - c)], s_c + k, azi=azi).wait_recv()
        wire.copy(w, w_all.at[index(1 - x, (z + NZ - k) % NZ, 1 - c)], s_c + NZ + k,
                  azi=azi).wait_recv()
    for k in range(NZ):
        if k:
            along[k].wait_send()
        xs[k].wait_send()
        cs[k].wait_send()
        cs[NZ + k].wait_send()


def block_of(acc, at, deep):
    return acc[pl.ds(pl.multiple_of(at * deep, deep), deep), :]


def sum_weights(wire, acc, low, gsum, share, gtot, r1, r2, s1, s2, r3, s3, r4, s4, gbuf, gz, gr,
                n_rad):
    rad, azi = wire.rad, wire.azi
    x, z, c = place(azi)
    across, partner = index(1 - x, z, c), index(x, z, 1 - c)
    s_c, s_x, s_z = wire.slot(2 * NZ), wire.slot(NZ), wire.slot(NZ)
    s_g = wire.slot(2)
    s_gz = wire.slot(NZ)
    order = FAR + (0,)
    deep = s4.shape[0]
    core = {}
    for half in (1, 0):
        for k in order:
            xx = (x + half) % NX
            zz = (z + k) % NZ
            low[half, k] = block_of(acc, index(xx, zz, 1 - c), deep).astype(BF16)
            core[half, k] = wire.copy(low.at[half, k], r1.at[half, k],
                                      s_c + half * NZ + k, azi=partner)
            core[half, k].start()
    g_core = wire.copy(gsum, gbuf.at[0], s_g, azi=partner)
    g_core.start()
    yield
    xs, zs = {}, {}
    for k in order:
        core[1, k].wait_recv()
        mine = block_of(acc, index(1 - x, (z + k) % NZ, c), deep)
        s1[k] = (mine + r1[1, k].astype(F32)).astype(BF16)
        xs[k] = wire.copy(s1.at[k], r2.at[k], s_x + k, azi=across)
        xs[k].start()
    g_core.wait_recv()
    gbuf[1] = gsum[...] + gbuf[0]
    g_x = wire.copy(gbuf.at[1], gbuf.at[2], s_g + 1, azi=across)
    g_x.start()
    yield
    for count, k in enumerate(order):
        core[0, k].wait_recv()
        xs[k].wait_recv()
        mine = block_of(acc, index(x, (z + k) % NZ, c), deep)
        total = mine + r1[0, k].astype(F32) + r2[k].astype(F32)
        s2[k] = total.astype(BF16)
        if k:
            zs[k] = wire.copy(s2.at[k], r3.at[k], s_z + k, azi=index(x, (z + k) % NZ, c))
            zs[k].start()
        if count % 3 == 2:
            yield
    g_x.wait_recv()
    gz[z] = gbuf[1] + gbuf[2]
    g_zs = {}
    for k in FAR:
        g_zs[k] = wire.copy(gz.at[z], gz.at[z], s_gz + k, azi=index(x, (z + k) % NZ, c))
        g_zs[k].start()
    yield
    total = s2[0].astype(F32)
    for k in (1, 7, 2, 6, 3, 5, 4):
        zs[k].wait_recv()
        total = total + r3[k].astype(F32)
    part = s4.shape[1]
    for g in range(n_rad):
        s3[g] = total[:, part * g: part * (g + 1)].astype(BF16)
    s_r, s_a, s_gr = wire.slot(n_rad), wire.slot(n_rad), wire.slot(n_rad)
    outs = []
    for k in range(1, n_rad):
        to = (rad + k) % n_rad
        copy = wire.copy(s3.at[to], r4.at[k], s_r + k, rad=to)
        copy.start()
        outs.append(copy)
    for k in FAR:
        wire.copy(gz.at[z], gz.at[(z + NZ - k) % NZ], s_gz + k, azi=azi).wait_recv()
    value = gz[0]
    for k in range(1, NZ):
        value = value + gz[k]
    gr[rad] = value
    g_outs = []
    for k in range(1, n_rad):
        copy = wire.copy(gr.at[rad], gr.at[rad], s_gr + k, rad=(rad + k) % n_rad)
        copy.start()
        g_outs.append(copy)
    yield
    total = s3[rad].astype(F32)
    for k in range(1, n_rad):
        outs[k - 1].wait_recv()
        total = total + r4[k].astype(F32)
    s4[...] = total.astype(BF16)
    share[rad] = s4[...]
    finals = []
    for k in range(1, n_rad):
        copy = wire.copy(s4, share.at[rad], s_a + k, rad=(rad + k) % n_rad)
        copy.start()
        finals.append(copy)
    yield
    for k in range(1, n_rad):
        wire.copy(gr.at[rad], gr.at[(rad + n_rad - k) % n_rad], s_gr + k, rad=rad).wait_recv()
    value = gr[0]
    for k in range(1, n_rad):
        value = value + gr[k]
    gtot[...] = value
    for k in range(1, n_rad):
        wire.copy(s4, share.at[(rad + n_rad - k) % n_rad], s_a + k, rad=rad).wait_recv()
    for copy in list(core.values()) + list(xs.values()) + list(zs.values()) + list(g_zs.values()):
        copy.wait_send()
    for copy in outs + g_outs + finals + [g_core, g_x]:
        copy.wait_send()


class Runs:
    def __init__(self):
        self.live = []

    def add(self, run):
        next(run)
        self.live.append(run)
        return run

    def tick(self, *runs):
        for run in runs:
            if run in self.live and next(run, self) is self:
                self.live.remove(run)

    def finish(self, *runs):
        while any(run in self.live for run in runs):
            self.tick(*runs)


COPIES = 192
GROUPS = 4
VM = pl.BlockSpec(memory_space=pltpu.VMEM)
SM = pl.BlockSpec(memory_space=pltpu.SMEM)
ANY = pl.BlockSpec(memory_space=pl.ANY)


def layer_kernel(n_rad, n_azi, shear, shift, tok, cot, gain_ref, wqkv_own, wout_own,
                 ext, share, gtot,
                 main, far, w_own, w_all, cur, got, five, stage, cur_b, got_b, five_b, stage_b,
                 frame, acc, gsum, qkv_t, dat_t, att_t, dqkv_t,
                 low, r1, r2, s1, s2, r3, s3, r4, s4, gbuf, gz, gr, send, recv):
    wire = Wire(send, recv)
    rad, azi = wire.rad, wire.azi
    rows, cols, depth, width = tok.shape
    srcs = (tok, cot)
    n = WR * WA * depth
    before, after = (azi + n_azi - 1) % n_azi, (azi + 1) % n_azi
    middle, left, right = pl.ds(SIDE, cols), pl.ds(0, SIDE), pl.ds(cols + SIDE, SIDE)
    s_local = wire.slot(4)
    here = [
        wire.local(wqkv_own, w_own.at[:, pl.ds(0, 3 * width)], s_local),
        wire.local(wout_own, w_own.at[:, pl.ds(3 * width, width)], s_local + 1),
        wire.local(tok, main.at[0, :, middle], s_local + 2),
        wire.local(cot, main.at[1, :, middle], s_local + 3),
    ]
    for copy in here:
        copy.start()
    shift_rad, shift_azi = shift[0], shift[1]
    total_cols = cols * n_azi
    lean = jnp.where(shift_azi > SIDE, shift_azi - WA, shift_azi)
    forth = lax.rem(shear[0] + lean + total_cols, jnp.int32(total_cols))
    back = lax.rem(total_cols - forth, jnp.int32(total_cols))

    acc[...] = jnp.zeros_like(acc)
    gsum[...] = jnp.zeros_like(gsum)
    greet(n_rad, n_azi)
    for copy in here[:2]:
        copy.wait()

    runs = Runs()
    weights = runs.add(gather_weights(wire, w_own, w_all.at[...]))
    s_side = wire.slot(4)
    sides = []
    for t in range(2):
        sides.append(wire.copy(srcs[t].at[:, pl.ds(0, SIDE)], main.at[t, :, right],
                               s_side + 2 * t, azi=before))
        sides.append(wire.copy(srcs[t].at[:, pl.ds(cols - SIDE, SIDE)], main.at[t, :, left],
                               s_side + 2 * t + 1, azi=after))
    for copy in sides:
        copy.start()
    quarters = n_rad // 2
    come = (
        runs.add(roll(
            wire,
            lambda g: srcs[g // quarters].at[pl.ds(0, RIM), :, :, lane_block(g % quarters)],
            0, n_rad - 1, forth,
            lambda t, f: far.at[t, :, pl.ds(0, cols), :, lane_block(f)],
            cur, got, five, stage, n_rad, n_azi)),
        runs.add(rims(wire, lambda t: srcs[t].at[pl.ds(0, RIM)], far, 0, n_rad - 1, -1, cols,
                      n_rad, n_azi)),
    )
    step = 0
    while weights in runs.live:
        runs.tick(weights)
        if step % 2 == 1:
            runs.tick(come[0])
        step += 1
    for copy in here[2:]:
        copy.wait()
    for copy in sides:
        copy.wait()

    gain = gain_ref[...]
    deep = w_own.shape[0]
    wqkv = w_all.reshape(n_azi * deep, 4 * width).at[:, pl.ds(0, 3 * width)]
    wout = w_all.reshape(n_azi * deep, 4 * width).at[:, pl.ds(3 * width, width)]
    scale = HD ** -0.5
    col_near = SIDE + lean
    col_far = jnp.where(rad == n_rad - 1, 0, col_near)

    def line(t, i, j, r):
        row = shift_rad + WR * i + r
        near = main[t, jnp.minimum(row, rows - 1), pl.ds(col_near + WA * j, WA)].astype(F32)
        if WR * i + r + RIM < rows:
            return near
        other = far[t, jnp.maximum(row - rows, 0), pl.ds(col_far + WA * j, WA)].astype(F32)
        if WR * i + r + 1 >= rows:
            return other
        return jnp.where(row < rows, near, other)

    def window(i, j, *plan):
        def load(t):
            return jnp.concatenate(
                [line(t, i, j, r).reshape(WA * depth, width) for r in range(WR)], axis=0)

        x = load(0)
        g = load(1)
        centred = x - jnp.mean(x, axis=1, keepdims=True)
        inv = lax.rsqrt(jnp.mean(centred * centred, axis=1, keepdims=True) + EPS)
        xhat = centred * inv
        hidden = (xhat * gain).astype(BF16)
        g_low = g.astype(BF16)
        qkv_t[...] = mm(hidden, wqkv[...]).T.astype(BF16)
        dat_t[...] = mm(g_low, wout[...], NT).T.astype(BF16)

        def head(h, carry):
            at = pl.multiple_of(h * HD, HD)
            q = qkv_t[pl.ds(at, HD), :]
            k = qkv_t[pl.ds(width + at, HD), :]
            v = qkv_t[pl.ds(2 * width + at, HD), :]
            d = dat_t[pl.ds(at, HD), :]
            s = mm(k, q, TN)
            e = jnp.exp((s - jnp.max(s, axis=0, keepdims=True)) * scale)
            p = e * (1.0 / jnp.sum(e, axis=0, keepdims=True))
            low_p = p.astype(BF16)
            att = mm(v, low_p)
            att_t[pl.ds(at, HD), :] = att.astype(BF16)
            dp = mm(v, d, TN)
            dot = jnp.sum(att * d.astype(F32), axis=0, keepdims=True)
            ds = (p * (dp - dot)).astype(BF16)
            dqkv_t[pl.ds(at, HD), :] = (mm(k, ds) * scale).astype(BF16)
            dqkv_t[pl.ds(width + at, HD), :] = (mm(q, ds, NT) * scale).astype(BF16)
            dqkv_t[pl.ds(2 * width + at, HD), :] = mm(d, low_p, NT).astype(BF16)
            return carry

        each = HEADS // GROUPS
        for group in range(GROUPS):
            lax.fori_loop(group * each, (group + 1) * each, head, 0, unroll=UNROLL)
            runs.tick(*(plan[group] if plan else ()))
        shape = (WR, WA, depth, width)
        own, at = pl.ds(WR * i, WR), pl.ds(WA * j, WA)
        att_all = att_t[...]
        frame[0, own, at] = (x + mm(att_all, wout[...], TN)).reshape(shape).astype(BF16)
        dqkv = dqkv_t[...]
        acc[:, : 3 * width] += mm(hidden, dqkv, TT)
        acc[:, 3 * width:] += mm(att_all, g_low)
        dh = mm(dqkv, wqkv[...], TT)
        gsum[...] += jnp.sum(dh * xhat, axis=0, keepdims=True)
        dx = dh * gain
        dx = inv * (dx - jnp.mean(dx, axis=1, keepdims=True)
                    - xhat * jnp.mean(dx * xhat, axis=1, keepdims=True))
        frame[1, own, at] = (g + dx).reshape(shape).astype(BF16)

    s_out = wire.slot(8)
    back_sides = {}
    for i in range(2):
        own = pl.ds(WR * i, WR)
        there = pl.ds(RIM + WR * i, WR)
        back_sides[i, 0] = wire.copy(frame.at[:, own, pl.ds(0, SIDE)], ext.at[:, there, right],
                                     s_out + 2 * i, azi=before)
        back_sides[i, 1] = wire.copy(frame.at[:, own, pl.ds(cols - SIDE, SIDE)],
                                     ext.at[:, there, left], s_out + 2 * i + 1, azi=after)
    window(0, 0, (), come[:1], (), come)
    back_sides[0, 0].start()
    runs.finish(*come)
    window(1, 0)
    window(1, 1)
    go = (
        runs.add(roll(
            wire,
            lambda g: frame.at[g // quarters, pl.ds(rows - RIM, RIM), :, :,
                               lane_block(g % quarters)],
            n_rad - 1, 0, back,
            lambda t, f: ext.at[t, pl.ds(0, RIM), pl.ds(0, cols), :, lane_block(f)],
            cur_b, got_b, five_b, stage_b, n_rad, n_azi)),
        runs.add(rims(wire, lambda t: frame.at[t, pl.ds(rows - RIM, RIM)],
                      ext.at[:, pl.ds(0, RIM)], n_rad - 1, 0, 1, cols, n_rad, n_azi)),
    )
    back_sides[1, 0].start()
    back_sides[1, 1].start()
    window(0, 1, (), go[:1], (), go[:1])
    back_sides[0, 1].start()
    final = [wire.local(frame.at[t], ext.at[t, pl.ds(RIM, rows), middle], s_out + 4 + t)
             for t in range(2)]
    for copy in final:
        copy.start()
    sums = runs.add(sum_weights(wire, acc, low, gsum, share, gtot, r1, r2, s1, s2, r3, s3, r4, s4, gbuf,
                         gz, gr, n_rad))
    step = 0
    while sums in runs.live:
        runs.tick(sums)
        if step % 2 == 1:
            runs.tick(*go[:1 + step // 3])
        step += 1
    runs.finish(*go)
    for copy in list(back_sides.values()) + final:
        copy.wait()


def layer(shear, shift, tok, cot, gain, wqkv, wout, n_rad, n_azi):
    rows, cols, depth, width = tok.shape
    deep, wide = wout.shape[0], 4 * width
    part = wide // n_rad
    n = WR * WA * depth
    across = cols + 2 * SIDE

    def kernel(*refs):
        layer_kernel(n_rad, n_azi, *refs)

    rolls = [
        pltpu.VMEM((2, RIM, cols, depth, LANES), BF16),
        pltpu.VMEM((4, RIM, cols, depth, LANES), BF16),
        pltpu.VMEM((RIM, 5 * cols, depth, LANES), BF16),
        pltpu.VMEM((RIM, cols, depth, LANES), BF16),
    ]
    return pl.pallas_call(
        kernel,
        out_shape=(
            jax.ShapeDtypeStruct((2, rows + RIM, across, depth, width), BF16),
            jax.ShapeDtypeStruct((n_rad, deep, part), BF16),
            jax.ShapeDtypeStruct((1, width), F32),
        ),
        in_specs=[SM, SM, ANY, ANY, VM, ANY, ANY],
        out_specs=(VM, VM, VM),
        scratch_shapes=[
            pltpu.VMEM((2, rows, across, depth, width), BF16),
            pltpu.VMEM((2, RIM, across, depth, width), BF16),
            pltpu.VMEM((deep, wide), BF16),
            pltpu.VMEM((n_azi, deep, wide), BF16),
        ] + rolls + rolls + [
            pltpu.VMEM((2, rows, cols, depth, width), BF16),
            pltpu.VMEM((width, wide), F32),
            pltpu.VMEM((1, width), F32),
            pltpu.VMEM((3 * width, n), BF16),
            pltpu.VMEM((width, n), BF16),
            pltpu.VMEM((width, n), BF16),
            pltpu.VMEM((3 * width, n), BF16),
            pltpu.VMEM((NX, NZ, deep, wide), BF16),
            pltpu.VMEM((NX, NZ, deep, wide), BF16),
            pltpu.VMEM((NZ, deep, wide), BF16),
            pltpu.VMEM((NZ, deep, wide), BF16),
            pltpu.VMEM((NZ, deep, wide), BF16),
            pltpu.VMEM((NZ, deep, wide), BF16),
            pltpu.VMEM((n_rad, deep, part), BF16),
            pltpu.VMEM((n_rad, deep, part), BF16),
            pltpu.VMEM((deep, part), BF16),
            pltpu.VMEM((3, 1, width), F32),
            pltpu.VMEM((NZ, 1, width), F32),
            pltpu.VMEM((n_rad, 1, width), F32),
            pltpu.SemaphoreType.DMA((COPIES,)),
            pltpu.SemaphoreType.DMA((COPIES,)),
        ],
        compiler_params=pltpu.CompilerParams(
            collective_id=0, has_side_effects=True, vmem_limit_bytes=VMEM_LIMIT),
    )(shear, shift, tok, cot, gain, wqkv, wout)


def settle_kernel(n_rad, shift, ext_ref, out_ref, grad_ref):
    rows, cols = out_ref.shape[:2]
    lean = jnp.where(shift[1] > SIDE, shift[1] - WA, shift[1])
    outer = SIDE - lean
    above = jnp.where(lax.axis_index("rad") == 0, 0, outer)
    for t, ref in enumerate((out_ref, grad_ref)):
        for r in range(rows):
            row = RIM - shift[0] + r
            first = jnp.where(row < RIM, above, outer)
            ref[r] = ext_ref[t, row, pl.ds(first, cols)]


def settle(shift, ext, rows, cols, n_rad):
    depth, width = ext.shape[3:]
    shape = jax.ShapeDtypeStruct((rows, cols, depth, width), BF16)

    def kernel(*refs):
        settle_kernel(n_rad, *refs)

    return pl.pallas_call(
        kernel,
        out_shape=(shape, shape),
        in_specs=[SM, VM],
        out_specs=(VM, VM),
        compiler_params=pltpu.CompilerParams(vmem_limit_bytes=VMEM_LIMIT),
    )(shift, ext)


def on_device(tokens, cotangent, ln_gain, qkv_weight, out_weight, shear_offset, window_shift):
    rows, cols, depth, width = tokens.shape
    n_rad, n_azi = lax.axis_size("rad"), lax.axis_size("azi")
    ext, share, gtot = layer(shear_offset, window_shift, tokens, cotangent,
                             ln_gain.reshape(1, width), qkv_weight, out_weight, n_rad, n_azi)
    block_out, grad_tokens = settle(window_shift, ext, rows, cols, n_rad)
    factor = float(rows * cols * depth * n_rad * n_azi) ** (-0.5)
    share = share.transpose(1, 0, 2).reshape(width // n_azi, 4 * width).astype(F32) * factor
    return (block_out, grad_tokens, share[:, : 3 * width], share[:, 3 * width:],
            gtot.reshape(width) * factor)


def solution(mesh):
    in_specs = (
        P("rad", "azi", None, None),
        P("rad", "azi", None, None),
        P(),
        P("azi", None),
        P("azi", None),
        P(),
        P(),
    )
    out_specs = (
        P("rad", "azi", None, None),
        P("rad", "azi", None, None),
        P("azi", None),
        P("azi", None),
        P(),
    )
    return jax.shard_map(
        on_device, mesh=mesh, in_specs=in_specs, out_specs=out_specs, check_vma=False
    )
```

```python
import jax
import jax.numpy as jnp
from jax import lax
from jax.experimental import pallas as pl
from jax.experimental.pallas import tpu as pltpu
from jax.sharding import PartitionSpec as P

HEADS = 16
HD = 32
WR = 4
WA = 8
RIM = WR - 1
SIDE = WA // 2
EPS = 1e-05
F32 = jnp.float32
BF16 = jnp.bfloat16
NN = (((1,), (0,)), ((), ()))
NT = (((1,), (1,)), ((), ()))
TN = (((0,), (0,)), ((), ()))
TT = (((0,), (1,)), ((), ()))
LANES = 128
NX, NZ, NC = 2, 8, 2
FAR = (4, 3, 5, 2, 6, 1, 7)
NEAR = (1, 7, 2, 6, 3, 5, 4)
UNROLL = 4
VMEM_LIMIT = 60 * 2 ** 20


def mm(a, b, dims=NN):
    return lax.dot_general(a, b, dims, preferred_element_type=F32)


class Wire:
    def __init__(self, send, recv):
        self.send, self.recv, self.used = send, recv, 0
        self.rad, self.azi = lax.axis_index("rad"), lax.axis_index("azi")
        self.waits = []

    def slot(self, count=1):
        first = self.used
        self.used += count
        return first

    def copy(self, src, dst, slot, rad=None, azi=None, recv_slot=None):
        rad = self.rad if rad is None else rad
        azi = self.azi if azi is None else azi
        return pltpu.make_async_remote_copy(
            src_ref=src,
            dst_ref=dst,
            send_sem=self.send.at[slot],
            recv_sem=self.recv.at[slot if recv_slot is None else recv_slot],
            device_id=(rad, azi),
            device_id_type=pl.DeviceIdType.MESH,
        )

    def local(self, src, dst, slot):
        return pltpu.make_async_copy(src, dst, self.recv.at[slot])


def greet(n_rad, n_azi):
    rad, azi = lax.axis_index("rad"), lax.axis_index("azi")
    barrier = pltpu.get_barrier_semaphore()
    for step in range(1, n_azi):
        pl.semaphore_signal(
            barrier, inc=1, device_id=(rad, (azi + step) % n_azi),
            device_id_type=pl.DeviceIdType.MESH)
    for step in range(1, n_rad):
        pl.semaphore_signal(
            barrier, inc=1, device_id=((rad + step) % n_rad, azi),
            device_id_type=pl.DeviceIdType.MESH)
    pl.semaphore_wait(barrier, n_azi + n_rad - 2)


def roll(wire, take, start, finish, amount, land, cur, got, five, stage, n_rad, n_azi):
    rad, azi = wire.rad, wire.azi
    cols = stage.shape[1]
    quarters = n_rad // 2
    coarse = (amount + 2 * cols) // (4 * cols)
    rem = amount + 2 * cols - 4 * cols * coarse
    coarse = coarse & 7
    s_scatter = wire.slot(n_rad)
    scatter = [
        wire.copy(take(g), cur.at[0], s_scatter + g, rad=g, recv_slot=s_scatter)
        for g in range(n_rad)
    ]
    scatter_own = wire.local(take(start), cur.at[0], s_scatter)

    @pl.when(rad == start)
    def _():
        for g in range(n_rad):
            if g != start:
                scatter[g].start()
        scatter_own.start()

    yield

    @pl.when(rad == start)
    def _():
        scatter_own.wait()

    @pl.when(rad != start)
    def _():
        scatter[start].wait_recv()

    s_hop = wire.slot(8)

    def hop(src, dst, number, distance):
        copy = wire.copy(src, dst, s_hop + number, azi=(azi + n_azi - distance) % n_azi)
        copy.start()
        return copy

    hops = [hop(cur.at[0], got.at[0], 0, n_azi // 2)]
    yield
    hops[0].wait_recv()
    cur[1] = jnp.where(coarse >= 4, got[0], cur[0])
    for k in (2, 1, 3):
        hops.append(hop(cur.at[1], got.at[k], k, 4 * k))
    yield
    for copy in hops[1:]:
        copy.wait_recv()
    fine = coarse & 3
    near = jnp.where(fine == 1, got[1], cur[1])
    other = jnp.where(fine == 2, got[2], got[3])
    five[:, pl.ds(2 * cols, cols)] = jnp.where(fine >= 2, other, near)
    for number, k in enumerate((2, -2, 1, -1)):
        hops.append(hop(five.at[:, pl.ds(2 * cols, cols)],
                        five.at[:, pl.ds((2 + k) * cols, cols)], 4 + number, k))
    yield
    for copy in hops[4:]:
        copy.wait_recv()
    stage[...] = five[:, pl.ds(rem, cols)]
    s_last = wire.slot(n_rad)
    last = wire.copy(stage, land(rad // quarters, rad % quarters), s_last, rad=finish,
                     recv_slot=s_last + rad)
    last_own = wire.local(stage, land(finish // quarters, finish % quarters), s_last + finish)

    @pl.when(rad == finish)
    def _():
        last_own.start()

    @pl.when(rad != finish)
    def _():
        last.start()

    yield
    for copy in hops:
        copy.wait_send()

    @pl.when(rad != finish)
    def _():
        last.wait_send()

    @pl.when(rad == finish)
    def _():
        last_own.wait()
        for g in range(n_rad):
            if g != finish:
                wire.copy(stage, land(g // quarters, g % quarters), s_last, rad=finish,
                          recv_slot=s_last + g).wait_recv()

    @pl.when(rad == start)
    def _():
        for g in range(n_rad):
            if g != start:
                scatter[g].wait_send()


def rims(wire, take, far, start, finish, step_rad, cols, n_rad, n_azi):
    rad, azi = wire.rad, wire.azi
    before, after = (azi + n_azi - 1) % n_azi, (azi + 1) % n_azi
    middle = pl.ds(SIDE, cols)
    s_rim = wire.slot(2)
    moved = [
        wire.copy(take(t), far.at[t, :, middle], s_rim + t,
                  rad=(rad + step_rad + n_rad) % n_rad)
        for t in range(2)
    ]

    @pl.when(rad != start)
    def _():
        for copy in moved:
            copy.start()

    yield
    s_corner = wire.slot(2)
    corners = [
        wire.copy(far.at[:, :, pl.ds(SIDE, SIDE)], far.at[:, :, pl.ds(cols + SIDE, SIDE)],
                  s_corner, azi=before),
        wire.copy(far.at[:, :, pl.ds(cols, SIDE)], far.at[:, :, pl.ds(0, SIDE)],
                  s_corner + 1, azi=after),
    ]

    @pl.when(rad != finish)
    def _():
        for copy in moved:
            copy.wait_recv()
        for copy in corners:
            copy.start()

    yield

    @pl.when(rad != finish)
    def _():
        for copy in corners:
            copy.wait()

    @pl.when(rad != start)
    def _():
        for copy in moved:
            copy.wait_send()


def lane_block(f):
    return pl.ds(pl.multiple_of(f * LANES, LANES), LANES)


def place(azi):
    return azi // (NZ * NC), azi // NC % NZ, azi % NC


def index(x, z, c):
    return (x * NZ + z) * NC + c


def gather_weights(wire, w, w_all):
    azi = wire.azi
    x, z, c = place(azi)
    across, partner = index(1 - x, z, c), index(x, z, 1 - c)
    s_own, s_z, s_x, s_c = wire.slot(), wire.slot(NZ), wire.slot(NZ), wire.slot(2 * NZ)
    own = wire.local(w, w_all.at[azi], s_own)
    own.start()
    sent = []
    along = {}
    for k in NEAR:
        along[k] = wire.copy(w, w_all.at[azi], s_z + k, azi=index(x, (z + k) % NZ, c))
        along[k].start()
    first = [
        wire.copy(w, w_all.at[azi], s_x, azi=across),
        wire.copy(w, w_all.at[azi], s_c, azi=partner),
    ]
    for copy in first:
        copy.start()
    yield
    xs, cs = {0: first[0]}, {0: first[1]}
    for count, k in enumerate(NEAR):
        came = index(x, (z + NZ - k) % NZ, c)
        wire.copy(w, w_all.at[came], s_z + k, azi=azi).wait_recv()
        xs[k] = wire.copy(w_all.at[came], w_all.at[came], s_x + k, azi=across)
        cs[k] = wire.copy(w_all.at[came], w_all.at[came], s_c + k, azi=partner)
        xs[k].start()
        cs[k].start()
        if count % 2 == 1:
            yield
    for count, k in enumerate((0,) + NEAR):
        came = index(1 - x, (z + NZ - k) % NZ, c)
        wire.copy(w, w_all.at[came], s_x + k, azi=azi).wait_recv()
        cs[NZ + k] = wire.copy(w_all.at[came], w_all.at[came], s_c + NZ + k, azi=partner)
        cs[NZ + k].start()
        if count % 3 == 2:
            yield
    own.wait()
    for k in range(NZ):
        wire.copy(w, w_all.at[index(x, (z + NZ - k) % NZ, 1 - c)], s_c + k, azi=azi).wait_recv()
        wire.copy(w, w_all.at[index(1 - x, (z + NZ - k) % NZ, 1 - c)], s_c + NZ + k,
                  azi=azi).wait_recv()
    for k in range(NZ):
        if k:
            along[k].wait_send()
        xs[k].wait_send()
        cs[k].wait_send()
        cs[NZ + k].wait_send()


def block_of(acc, at, deep):
    return acc[pl.ds(pl.multiple_of(at * deep, deep), deep), :]


def sum_weights(wire, acc, low, gsum, share, gtot, r1, r2, s1, s2, r3, s3, r4, s4, gbuf, gz, gr,
                n_rad):
    rad, azi = wire.rad, wire.azi
    x, z, c = place(azi)
    across, partner = index(1 - x, z, c), index(x, z, 1 - c)
    s_c, s_x, s_z = wire.slot(2 * NZ), wire.slot(NZ), wire.slot(NZ)
    s_g = wire.slot(2)
    s_gz = wire.slot(NZ)
    order = FAR + (0,)
    deep = s4.shape[0]
    core = {}
    for half in (1, 0):
        for k in order:
            xx = (x + half) % NX
            zz = (z + k) % NZ
            low[half, k] = block_of(acc, index(xx, zz, 1 - c), deep).astype(BF16)
            core[half, k] = wire.copy(low.at[half, k], r1.at[half, k],
                                      s_c + half * NZ + k, azi=partner)
            core[half, k].start()
    g_core = wire.copy(gsum, gbuf.at[0], s_g, azi=partner)
    g_core.start()
    yield
    xs, zs = {}, {}
    for k in order:
        core[1, k].wait_recv()
        mine = block_of(acc, index(1 - x, (z + k) % NZ, c), deep)
        s1[k] = (mine + r1[1, k].astype(F32)).astype(BF16)
        xs[k] = wire.copy(s1.at[k], r2.at[k], s_x + k, azi=across)
        xs[k].start()
    g_core.wait_recv()
    gbuf[1] = gsum[...] + gbuf[0]
    g_x = wire.copy(gbuf.at[1], gbuf.at[2], s_g + 1, azi=across)
    g_x.start()
    yield
    for count, k in enumerate(order):
        core[0, k].wait_recv()
        xs[k].wait_recv()
        mine = block_of(acc, index(x, (z + k) % NZ, c), deep)
        total = mine + r1[0, k].astype(F32) + r2[k].astype(F32)
        s2[k] = total.astype(BF16)
        if k:
            zs[k] = wire.copy(s2.at[k], r3.at[k], s_z + k, azi=index(x, (z + k) % NZ, c))
            zs[k].start()
        if count % 3 == 2:
            yield
    g_x.wait_recv()
    gz[z] = gbuf[1] + gbuf[2]
    g_zs = {}
    for k in FAR:
        g_zs[k] = wire.copy(gz.at[z], gz.at[z], s_gz + k, azi=index(x, (z + k) % NZ, c))
        g_zs[k].start()
    yield
    total = s2[0].astype(F32)
    for k in NEAR:
        zs[k].wait_recv()
        total = total + r3[k].astype(F32)
    part = s4.shape[1]
    for g in range(n_rad):
        s3[g] = total[:, part * g: part * (g + 1)].astype(BF16)
    s_r, s_a, s_gr = wire.slot(n_rad), wire.slot(n_rad), wire.slot(n_rad)
    outs = []
    for k in range(1, n_rad):
        to = (rad + k) % n_rad
        copy = wire.copy(s3.at[to], r4.at[k], s_r + k, rad=to)
        copy.start()
        outs.append(copy)
    for k in FAR:
        wire.copy(gz.at[z], gz.at[(z + NZ - k) % NZ], s_gz + k, azi=azi).wait_recv()
    value = gz[0]
    for k in range(1, NZ):
        value = value + gz[k]
    gr[rad] = value
    g_outs = []
    for k in range(1, n_rad):
        copy = wire.copy(gr.at[rad], gr.at[rad], s_gr + k, rad=(rad + k) % n_rad)
        copy.start()
        g_outs.append(copy)
    yield
    total = s3[rad].astype(F32)
    for k in range(1, n_rad):
        outs[k - 1].wait_recv()
        total = total + r4[k].astype(F32)
    s4[...] = total.astype(BF16)
    share[rad] = s4[...]
    finals = []
    for k in range(1, n_rad):
        copy = wire.copy(s4, share.at[rad], s_a + k, rad=(rad + k) % n_rad)
        copy.start()
        finals.append(copy)
    yield
    for k in range(1, n_rad):
        wire.copy(gr.at[rad], gr.at[(rad + n_rad - k) % n_rad], s_gr + k, rad=rad).wait_recv()
    value = gr[0]
    for k in range(1, n_rad):
        value = value + gr[k]
    gtot[...] = value
    for k in range(1, n_rad):
        wire.copy(s4, share.at[(rad + n_rad - k) % n_rad], s_a + k, rad=rad).wait_recv()
    for copy in list(core.values()) + list(xs.values()) + list(zs.values()) + list(g_zs.values()):
        copy.wait_send()
    for copy in outs + g_outs + finals + [g_core, g_x]:
        copy.wait_send()


class Runs:
    def __init__(self):
        self.live = []

    def add(self, run):
        next(run)
        self.live.append(run)
        return run

    def tick(self, *runs):
        for run in runs:
            if run in self.live and next(run, self) is self:
                self.live.remove(run)

    def finish(self, *runs):
        while any(run in self.live for run in runs):
            self.tick(*runs)


COPIES = 192
GROUPS = 2
VM = pl.BlockSpec(memory_space=pltpu.VMEM)
SM = pl.BlockSpec(memory_space=pltpu.SMEM)
ANY = pl.BlockSpec(memory_space=pl.ANY)


def layer_kernel(n_rad, n_azi, shear, shift, tok, cot, gain_ref, wqkv_own, wout_own,
                 block_out, grad_out, share, gtot,
                 ext, main, far, w_own, w_all, cur, got, five, stage, cur_b, got_b, five_b, stage_b,
                 frame, acc, gsum, qkv_t, dat_t, att_t, dqkv_t,
                 low, r1, r2, s1, s2, r3, s3, r4, s4, gbuf, gz, gr, send, recv):
    wire = Wire(send, recv)
    rad, azi = wire.rad, wire.azi
    rows, cols, depth, width = tok.shape
    srcs = (tok, cot)
    n = WR * WA * depth
    before, after = (azi + n_azi - 1) % n_azi, (azi + 1) % n_azi
    middle, left, right = pl.ds(SIDE, cols), pl.ds(0, SIDE), pl.ds(cols + SIDE, SIDE)
    s_local = wire.slot(4)
    here = [
        wire.local(wqkv_own, w_own.at[:, pl.ds(0, 3 * width)], s_local),
        wire.local(wout_own, w_own.at[:, pl.ds(3 * width, width)], s_local + 1),
        wire.local(tok, main.at[0, :, middle], s_local + 2),
        wire.local(cot, main.at[1, :, middle], s_local + 3),
    ]
    for copy in here:
        copy.start()
    shift_rad, shift_azi = shift[0], shift[1]
    total_cols = cols * n_azi
    lean = jnp.where(shift_azi > SIDE, shift_azi - WA, shift_azi)
    forth = lax.rem(shear[0] + lean + total_cols, jnp.int32(total_cols))
    back = lax.rem(total_cols - forth, jnp.int32(total_cols))

    acc[...] = jnp.zeros_like(acc)
    gsum[...] = jnp.zeros_like(gsum)
    greet(n_rad, n_azi)
    for copy in here[:2]:
        copy.wait()

    runs = Runs()
    weights = runs.add(gather_weights(wire, w_own, w_all.at[...]))
    s_side = wire.slot(4)
    sides = []
    for t in range(2):
        sides.append(wire.copy(srcs[t].at[:, pl.ds(0, SIDE)], main.at[t, :, right],
                               s_side + 2 * t, azi=before))
        sides.append(wire.copy(srcs[t].at[:, pl.ds(cols - SIDE, SIDE)], main.at[t, :, left],
                               s_side + 2 * t + 1, azi=after))
    for copy in sides:
        copy.start()
    quarters = n_rad // 2
    come = (
        runs.add(roll(
            wire,
            lambda g: srcs[g // quarters].at[pl.ds(0, RIM), :, :, lane_block(g % quarters)],
            0, n_rad - 1, forth,
            lambda t, f: far.at[t, :, pl.ds(0, cols), :, lane_block(f)],
            cur, got, five, stage, n_rad, n_azi)),
        runs.add(rims(wire, lambda t: srcs[t].at[pl.ds(0, RIM)], far, 0, n_rad - 1, -1, cols,
                      n_rad, n_azi)),
    )
    step = 0
    while weights in runs.live:
        runs.tick(weights)
        if step % 2 == 1:
            runs.tick(come[0])
        step += 1
    for copy in here[2:]:
        copy.wait()
    for copy in sides:
        copy.wait()

    gain = gain_ref[...]
    deep = w_own.shape[0]
    wqkv = w_all.reshape(n_azi * deep, 4 * width).at[:, pl.ds(0, 3 * width)]
    wout = w_all.reshape(n_azi * deep, 4 * width).at[:, pl.ds(3 * width, width)]
    scale = HD ** -0.5
    col_near = SIDE + lean
    col_far = jnp.where(rad == n_rad - 1, 0, col_near)

    def line(t, i, j, r):
        row = shift_rad + WR * i + r
        near = main[t, jnp.minimum(row, rows - 1), pl.ds(col_near + WA * j, WA)].astype(F32)
        if WR * i + r + RIM < rows:
            return near
        other = far[t, jnp.maximum(row - rows, 0), pl.ds(col_far + WA * j, WA)].astype(F32)
        if WR * i + r + 1 >= rows:
            return other
        return jnp.where(row < rows, near, other)

    def window(i, j, *plan):
        def load(t):
            return jnp.concatenate(
                [line(t, i, j, r).reshape(WA * depth, width) for r in range(WR)], axis=0)

        x = load(0)
        g = load(1)
        centred = x - jnp.mean(x, axis=1, keepdims=True)
        inv = lax.rsqrt(jnp.mean(centred * centred, axis=1, keepdims=True) + EPS)
        xhat = centred * inv
        hidden = (xhat * gain).astype(BF16)
        g_low = g.astype(BF16)
        qkv_t[...] = mm(hidden, wqkv[...]).T.astype(BF16)
        dat_t[...] = mm(g_low, wout[...], NT).T.astype(BF16)

        def head(h, carry):
            at = pl.multiple_of(h * HD, HD)
            q = qkv_t[pl.ds(at, HD), :]
            k = qkv_t[pl.ds(width + at, HD), :]
            v = qkv_t[pl.ds(2 * width + at, HD), :]
            d = dat_t[pl.ds(at, HD), :]
            s = mm(k, q, TN)
            e = jnp.exp((s - jnp.max(s, axis=0, keepdims=True)) * scale)
            p = e * (1.0 / jnp.sum(e, axis=0, keepdims=True))
            low_p = p.astype(BF16)
            att = mm(v, low_p)
            att_t[pl.ds(at, HD), :] = att.astype(BF16)
            dp = mm(v, d, TN)
            dot = jnp.sum(att * d.astype(F32), axis=0, keepdims=True)
            ds = (p * (dp - dot)).astype(BF16)
            dqkv_t[pl.ds(at, HD), :] = (mm(k, ds) * scale).astype(BF16)
            dqkv_t[pl.ds(width + at, HD), :] = (mm(q, ds, NT) * scale).astype(BF16)
            dqkv_t[pl.ds(2 * width + at, HD), :] = mm(d, low_p, NT).astype(BF16)
            return carry

        each = HEADS // GROUPS
        for group in range(GROUPS):
            lax.fori_loop(group * each, (group + 1) * each, head, 0, unroll=UNROLL)
            runs.tick(*(plan[group] if plan else ()))
        shape = (WR, WA, depth, width)
        own, at = pl.ds(WR * i, WR), pl.ds(WA * j, WA)
        att_all = att_t[...]
        frame[0, own, at] = (x + mm(att_all, wout[...], TN)).reshape(shape).astype(BF16)
        dqkv = dqkv_t[...]
        acc[:, : 3 * width] += mm(hidden, dqkv, TT)
        acc[:, 3 * width:] += mm(att_all, g_low)
        dh = mm(dqkv, wqkv[...], TT)
        gsum[...] += jnp.sum(dh * xhat, axis=0, keepdims=True)
        dx = dh * gain
        dx = inv * (dx - jnp.mean(dx, axis=1, keepdims=True)
                    - xhat * jnp.mean(dx * xhat, axis=1, keepdims=True))
        frame[1, own, at] = (g + dx).reshape(shape).astype(BF16)

    s_out = wire.slot(8)
    back_sides = {}
    for i in range(2):
        own = pl.ds(WR * i, WR)
        there = pl.ds(RIM + WR * i, WR)
        back_sides[i, 0] = wire.copy(frame.at[:, own, pl.ds(0, SIDE)], ext.at[:, there, right],
                                     s_out + 2 * i, azi=before)
        back_sides[i, 1] = wire.copy(frame.at[:, own, pl.ds(cols - SIDE, SIDE)],
                                     ext.at[:, there, left], s_out + 2 * i + 1, azi=after)
    window(0, 0, come[:1], come)
    back_sides[0, 0].start()
    runs.finish(*come)
    window(1, 0)
    window(1, 1)
    go = (
        runs.add(roll(
            wire,
            lambda g: frame.at[g // quarters, pl.ds(rows - RIM, RIM), :, :,
                               lane_block(g % quarters)],
            n_rad - 1, 0, back,
            lambda t, f: ext.at[t, pl.ds(0, RIM), pl.ds(0, cols), :, lane_block(f)],
            cur_b, got_b, five_b, stage_b, n_rad, n_azi)),
        runs.add(rims(wire, lambda t: frame.at[t, pl.ds(rows - RIM, RIM)],
                      ext.at[:, pl.ds(0, RIM)], n_rad - 1, 0, 1, cols, n_rad, n_azi)),
    )
    back_sides[1, 0].start()
    back_sides[1, 1].start()
    window(0, 1, go[:1], go[:1])
    back_sides[0, 1].start()
    final = [wire.local(frame.at[t], ext.at[t, pl.ds(RIM, rows), middle], s_out + 4 + t)
             for t in range(2)]
    for copy in final:
        copy.start()
    sums = runs.add(sum_weights(wire, acc, low, gsum, share, gtot, r1, r2, s1, s2, r3, s3, r4, s4, gbuf,
                         gz, gr, n_rad))
    step = 0
    while sums in runs.live:
        runs.tick(sums)
        if step % 2 == 1:
            runs.tick(*go[:1 + step // 3])
        step += 1
    runs.finish(*go)
    for copy in list(back_sides.values()) + final:
        copy.wait()
    outer = SIDE - lean
    above = jnp.where(rad == 0, 0, outer)
    for t, ref in enumerate((block_out, grad_out)):
        for r in range(rows):
            row = RIM - shift_rad + r
            first = jnp.where(row < RIM, above, outer)
            ref[r] = ext[t, row, pl.ds(first, cols)]


def layer(shear, shift, tok, cot, gain, wqkv, wout, n_rad, n_azi):
    rows, cols, depth, width = tok.shape
    deep, wide = wout.shape[0], 4 * width
    part = wide // n_rad
    n = WR * WA * depth
    across = cols + 2 * SIDE

    def kernel(*refs):
        layer_kernel(n_rad, n_azi, *refs)

    rolls = [
        pltpu.VMEM((2, RIM, cols, depth, LANES), BF16),
        pltpu.VMEM((4, RIM, cols, depth, LANES), BF16),
        pltpu.VMEM((RIM, 5 * cols, depth, LANES), BF16),
        pltpu.VMEM((RIM, cols, depth, LANES), BF16),
    ]
    return pl.pallas_call(
        kernel,
        out_shape=(
            jax.ShapeDtypeStruct(tok.shape, BF16),
            jax.ShapeDtypeStruct(tok.shape, BF16),
            jax.ShapeDtypeStruct((n_rad, deep, part), BF16),
            jax.ShapeDtypeStruct((1, width), F32),
        ),
        in_specs=[SM, SM, ANY, ANY, VM, ANY, ANY],
        out_specs=(VM, VM, VM, VM),
        scratch_shapes=[
            pltpu.VMEM((2, rows + RIM, across, depth, width), BF16),
            pltpu.VMEM((2, rows, across, depth, width), BF16),
            pltpu.VMEM((2, RIM, across, depth, width), BF16),
            pltpu.VMEM((deep, wide), BF16),
            pltpu.VMEM((n_azi, deep, wide), BF16),
        ] + rolls + rolls + [
            pltpu.VMEM((2, rows, cols, depth, width), BF16),
            pltpu.VMEM((width, wide), F32),
            pltpu.VMEM((1, width), F32),
            pltpu.VMEM((3 * width, n), BF16),
            pltpu.VMEM((width, n), BF16),
            pltpu.VMEM((width, n), BF16),
            pltpu.VMEM((3 * width, n), BF16),
            pltpu.VMEM((NX, NZ, deep, wide), BF16),
            pltpu.VMEM((NX, NZ, deep, wide), BF16),
            pltpu.VMEM((NZ, deep, wide), BF16),
            pltpu.VMEM((NZ, deep, wide), BF16),
            pltpu.VMEM((NZ, deep, wide), BF16),
            pltpu.VMEM((NZ, deep, wide), BF16),
            pltpu.VMEM((n_rad, deep, part), BF16),
            pltpu.VMEM((n_rad, deep, part), BF16),
            pltpu.VMEM((deep, part), BF16),
            pltpu.VMEM((3, 1, width), F32),
            pltpu.VMEM((NZ, 1, width), F32),
            pltpu.VMEM((n_rad, 1, width), F32),
            pltpu.SemaphoreType.DMA((COPIES,)),
            pltpu.SemaphoreType.DMA((COPIES,)),
        ],
        compiler_params=pltpu.CompilerParams(
            collective_id=0, has_side_effects=True, vmem_limit_bytes=VMEM_LIMIT),
    )(shear, shift, tok, cot, gain, wqkv, wout)


def on_device(tokens, cotangent, ln_gain, qkv_weight, out_weight, shear_offset, window_shift):
    rows, cols, depth, width = tokens.shape
    n_rad, n_azi = lax.axis_size("rad"), lax.axis_size("azi")
    block_out, grad_tokens, share, gtot = layer(
        shear_offset, window_shift, tokens, cotangent, ln_gain.reshape(1, width), qkv_weight,
        out_weight, n_rad, n_azi)
    factor = float(rows * cols * depth * n_rad * n_azi) ** (-0.5)
    share = share.transpose(1, 0, 2).reshape(width // n_azi, 4 * width).astype(F32) * factor
    return (block_out, grad_tokens, share[:, : 3 * width], share[:, 3 * width:],
            gtot.reshape(width) * factor)


def solution(mesh):
    in_specs = (
        P("rad", "azi", None, None),
        P("rad", "azi", None, None),
        P(),
        P("azi", None),
        P("azi", None),
        P(),
        P(),
    )
    out_specs = (
        P("rad", "azi", None, None),
        P("rad", "azi", None, None),
        P("azi", None),
        P("azi", None),
        P(),
    )
    return jax.shard_map(
        on_device, mesh=mesh, in_specs=in_specs, out_specs=out_specs, check_vma=False
    )
```

```python
import jax
import jax.numpy as jnp
from jax import lax
from jax.experimental import pallas as pl
from jax.experimental.pallas import tpu as pltpu
from jax.sharding import PartitionSpec as P

HEADS = 16
HD = 32
WR = 4
WA = 8
RIM = WR - 1
SIDE = WA // 2
EPS = 1e-05
F32 = jnp.float32
BF16 = jnp.bfloat16
NN = (((1,), (0,)), ((), ()))
NT = (((1,), (1,)), ((), ()))
TN = (((0,), (0,)), ((), ()))
TT = (((0,), (1,)), ((), ()))
LANES = 128
LOG2E = 1.4426950408889634
NX, NZ, NC = 2, 8, 2
FAR = (4, 3, 5, 2, 6, 1, 7)
NEAR = (1, 7, 2, 6, 3, 5, 4)
UNROLL = 4
VMEM_LIMIT = 60 * 2 ** 20


def mm(a, b, dims=NN):
    return lax.dot_general(a, b, dims, preferred_element_type=F32)


class Wire:
    def __init__(self, send, recv):
        self.send, self.recv, self.used = send, recv, 0
        self.rad, self.azi = lax.axis_index("rad"), lax.axis_index("azi")
        self.waits = []

    def slot(self, count=1):
        first = self.used
        self.used += count
        return first

    def copy(self, src, dst, slot, rad=None, azi=None, recv_slot=None):
        rad = self.rad if rad is None else rad
        azi = self.azi if azi is None else azi
        return pltpu.make_async_remote_copy(
            src_ref=src,
            dst_ref=dst,
            send_sem=self.send.at[slot],
            recv_sem=self.recv.at[slot if recv_slot is None else recv_slot],
            device_id=(rad, azi),
            device_id_type=pl.DeviceIdType.MESH,
        )

    def local(self, src, dst, slot):
        return pltpu.make_async_copy(src, dst, self.recv.at[slot])


def greet(n_rad, n_azi):
    rad, azi = lax.axis_index("rad"), lax.axis_index("azi")
    barrier = pltpu.get_barrier_semaphore()
    for step in range(1, n_azi):
        pl.semaphore_signal(
            barrier, inc=1, device_id=(rad, (azi + step) % n_azi),
            device_id_type=pl.DeviceIdType.MESH)
    for step in range(1, n_rad):
        pl.semaphore_signal(
            barrier, inc=1, device_id=((rad + step) % n_rad, azi),
            device_id_type=pl.DeviceIdType.MESH)
    pl.semaphore_wait(barrier, n_azi + n_rad - 2)


def roll(wire, take, start, finish, amount, land, cur, got, five, stage, n_rad, n_azi):
    rad, azi = wire.rad, wire.azi
    cols = stage.shape[1]
    quarters = n_rad // 2
    coarse = (amount + 2 * cols) // (4 * cols)
    rem = amount + 2 * cols - 4 * cols * coarse
    coarse = coarse & 7
    s_scatter = wire.slot(n_rad)
    scatter = [
        wire.copy(take(g), cur.at[0], s_scatter + g, rad=g, recv_slot=s_scatter)
        for g in range(n_rad)
    ]
    scatter_own = wire.local(take(start), cur.at[0], s_scatter)

    @pl.when(rad == start)
    def _():
        for g in range(n_rad):
            if g != start:
                scatter[g].start()
        scatter_own.start()

    yield

    @pl.when(rad == start)
    def _():
        scatter_own.wait()

    @pl.when(rad != start)
    def _():
        scatter[start].wait_recv()

    s_hop = wire.slot(8)

    def hop(src, dst, number, distance):
        copy = wire.copy(src, dst, s_hop + number, azi=(azi + n_azi - distance) % n_azi)
        copy.start()
        return copy

    hops = [hop(cur.at[0], got.at[0], 0, n_azi // 2)]
    yield
    hops[0].wait_recv()
    cur[1] = jnp.where(coarse >= 4, got[0], cur[0])
    for k in (2, 1, 3):
        hops.append(hop(cur.at[1], got.at[k], k, 4 * k))
    yield
    for copy in hops[1:]:
        copy.wait_recv()
    fine = coarse & 3
    near = jnp.where(fine == 1, got[1], cur[1])
    other = jnp.where(fine == 2, got[2], got[3])
    five[:, pl.ds(2 * cols, cols)] = jnp.where(fine >= 2, other, near)
    for number, k in enumerate((2, -2, 1, -1)):
        hops.append(hop(five.at[:, pl.ds(2 * cols, cols)],
                        five.at[:, pl.ds((2 + k) * cols, cols)], 4 + number, k))
    yield
    for copy in hops[4:]:
        copy.wait_recv()
    stage[...] = five[:, pl.ds(rem, cols)]
    s_last = wire.slot(n_rad)
    last = wire.copy(stage, land(rad // quarters, rad % quarters), s_last, rad=finish,
                     recv_slot=s_last + rad)
    last_own = wire.local(stage, land(finish // quarters, finish % quarters), s_last + finish)

    @pl.when(rad == finish)
    def _():
        last_own.start()

    @pl.when(rad != finish)
    def _():
        last.start()

    yield
    for copy in hops:
        copy.wait_send()

    @pl.when(rad != finish)
    def _():
        last.wait_send()

    @pl.when(rad == finish)
    def _():
        last_own.wait()
        for g in range(n_rad):
            if g != finish:
                wire.copy(stage, land(g // quarters, g % quarters), s_last, rad=finish,
                          recv_slot=s_last + g).wait_recv()

    @pl.when(rad == start)
    def _():
        for g in range(n_rad):
            if g != start:
                scatter[g].wait_send()


def rims(wire, take, far, start, finish, step_rad, cols, n_rad, n_azi):
    rad, azi = wire.rad, wire.azi
    before, after = (azi + n_azi - 1) % n_azi, (azi + 1) % n_azi
    middle = pl.ds(SIDE, cols)
    s_rim = wire.slot(2)
    moved = [
        wire.copy(take(t), far.at[t, :, middle], s_rim + t,
                  rad=(rad + step_rad + n_rad) % n_rad)
        for t in range(2)
    ]

    @pl.when(rad != start)
    def _():
        for copy in moved:
            copy.start()

    yield
    s_corner = wire.slot(2)
    corners = [
        wire.copy(far.at[:, :, pl.ds(SIDE, SIDE)], far.at[:, :, pl.ds(cols + SIDE, SIDE)],
                  s_corner, azi=before),
        wire.copy(far.at[:, :, pl.ds(cols, SIDE)], far.at[:, :, pl.ds(0, SIDE)],
                  s_corner + 1, azi=after),
    ]

    @pl.when(rad != finish)
    def _():
        for copy in moved:
            copy.wait_recv()
        for copy in corners:
            copy.start()

    yield

    @pl.when(rad != finish)
    def _():
        for copy in corners:
            copy.wait()

    @pl.when(rad != start)
    def _():
        for copy in moved:
            copy.wait_send()


def lane_block(f):
    return pl.ds(pl.multiple_of(f * LANES, LANES), LANES)


def place(azi):
    return azi // (NZ * NC), azi // NC % NZ, azi % NC


def index(x, z, c):
    return (x * NZ + z) * NC + c


def gather_weights(wire, w, w_all):
    azi = wire.azi
    x, z, c = place(azi)
    across, partner = index(1 - x, z, c), index(x, z, 1 - c)
    s_own, s_z, s_x, s_c = wire.slot(), wire.slot(NZ), wire.slot(NZ), wire.slot(2 * NZ)
    own = wire.local(w, w_all.at[azi], s_own)
    own.start()
    sent = []
    along = {}
    for k in NEAR:
        along[k] = wire.copy(w, w_all.at[azi], s_z + k, azi=index(x, (z + k) % NZ, c))
        along[k].start()
    first = [
        wire.copy(w, w_all.at[azi], s_x, azi=across),
        wire.copy(w, w_all.at[azi], s_c, azi=partner),
    ]
    for copy in first:
        copy.start()
    yield
    xs, cs = {0: first[0]}, {0: first[1]}
    for count, k in enumerate(NEAR):
        came = index(x, (z + NZ - k) % NZ, c)
        wire.copy(w, w_all.at[came], s_z + k, azi=azi).wait_recv()
        xs[k] = wire.copy(w_all.at[came], w_all.at[came], s_x + k, azi=across)
        cs[k] = wire.copy(w_all.at[came], w_all.at[came], s_c + k, azi=partner)
        xs[k].start()
        cs[k].start()
        if count % 2 == 1:
            yield
    for count, k in enumerate((0,) + NEAR):
        came = index(1 - x, (z + NZ - k) % NZ, c)
        wire.copy(w, w_all.at[came], s_x + k, azi=azi).wait_recv()
        cs[NZ + k] = wire.copy(w_all.at[came], w_all.at[came], s_c + NZ + k, azi=partner)
        cs[NZ + k].start()
        if count % 3 == 2:
            yield
    own.wait()
    for k in range(NZ):
        wire.copy(w, w_all.at[index(x, (z + NZ - k) % NZ, 1 - c)], s_c + k, azi=azi).wait_recv()
        wire.copy(w, w_all.at[index(1 - x, (z + NZ - k) % NZ, 1 - c)], s_c + NZ + k,
                  azi=azi).wait_recv()
    for k in range(NZ):
        if k:
            along[k].wait_send()
        xs[k].wait_send()
        cs[k].wait_send()
        cs[NZ + k].wait_send()


def block_of(acc, at, deep):
    return acc[pl.ds(pl.multiple_of(at * deep, deep), deep), :]


def sum_weights(wire, acc, low, gsum, share, gtot, r1, r2, s1, s2, r3, s3, r4, s4, gbuf, gz, gr,
                n_rad):
    rad, azi = wire.rad, wire.azi
    x, z, c = place(azi)
    across, partner = index(1 - x, z, c), index(x, z, 1 - c)
    s_c, s_x, s_z = wire.slot(2 * NZ), wire.slot(NZ), wire.slot(NZ)
    s_g = wire.slot(2)
    s_gz = wire.slot(NZ)
    order = FAR + (0,)
    deep = s4.shape[0]
    core = {}
    for half in (1, 0):
        for k in order:
            xx = (x + half) % NX
            zz = (z + k) % NZ
            low[half, k] = block_of(acc, index(xx, zz, 1 - c), deep).astype(BF16)
            core[half, k] = wire.copy(low.at[half, k], r1.at[half, k],
                                      s_c + half * NZ + k, azi=partner)
            core[half, k].start()
    g_core = wire.copy(gsum, gbuf.at[0], s_g, azi=partner)
    g_core.start()
    yield
    xs, zs = {}, {}
    for k in order:
        core[1, k].wait_recv()
        mine = block_of(acc, index(1 - x, (z + k) % NZ, c), deep)
        s1[k] = (mine + r1[1, k].astype(F32)).astype(BF16)
        xs[k] = wire.copy(s1.at[k], r2.at[k], s_x + k, azi=across)
        xs[k].start()
    g_core.wait_recv()
    gbuf[1] = gsum[...] + gbuf[0]
    g_x = wire.copy(gbuf.at[1], gbuf.at[2], s_g + 1, azi=across)
    g_x.start()
    yield
    for count, k in enumerate(order):
        core[0, k].wait_recv()
        xs[k].wait_recv()
        mine = block_of(acc, index(x, (z + k) % NZ, c), deep)
        total = mine + r1[0, k].astype(F32) + r2[k].astype(F32)
        s2[k] = total.astype(BF16)
        if k:
            zs[k] = wire.copy(s2.at[k], r3.at[k], s_z + k, azi=index(x, (z + k) % NZ, c))
            zs[k].start()
        if count % 3 == 2:
            yield
    g_x.wait_recv()
    gz[z] = gbuf[1] + gbuf[2]
    g_zs = {}
    for k in FAR:
        g_zs[k] = wire.copy(gz.at[z], gz.at[z], s_gz + k, azi=index(x, (z + k) % NZ, c))
        g_zs[k].start()
    yield
    total = s2[0].astype(F32)
    for k in NEAR:
        zs[k].wait_recv()
        total = total + r3[k].astype(F32)
    part = s4.shape[1]
    for g in range(n_rad):
        s3[g] = total[:, part * g: part * (g + 1)].astype(BF16)
    s_r, s_a, s_gr = wire.slot(n_rad), wire.slot(n_rad), wire.slot(n_rad)
    outs = []
    for k in range(1, n_rad):
        to = (rad + k) % n_rad
        copy = wire.copy(s3.at[to], r4.at[k], s_r + k, rad=to)
        copy.start()
        outs.append(copy)
    for k in FAR:
        wire.copy(gz.at[z], gz.at[(z + NZ - k) % NZ], s_gz + k, azi=azi).wait_recv()
    value = gz[0]
    for k in range(1, NZ):
        value = value + gz[k]
    gr[rad] = value
    g_outs = []
    for k in range(1, n_rad):
        copy = wire.copy(gr.at[rad], gr.at[rad], s_gr + k, rad=(rad + k) % n_rad)
        copy.start()
        g_outs.append(copy)
    yield
    total = s3[rad].astype(F32)
    for k in range(1, n_rad):
        outs[k - 1].wait_recv()
        total = total + r4[k].astype(F32)
    s4[...] = total.astype(BF16)
    share[rad] = s4[...]
    finals = []
    for k in range(1, n_rad):
        copy = wire.copy(s4, share.at[rad], s_a + k, rad=(rad + k) % n_rad)
        copy.start()
        finals.append(copy)
    yield
    for k in range(1, n_rad):
        wire.copy(gr.at[rad], gr.at[(rad + n_rad - k) % n_rad], s_gr + k, rad=rad).wait_recv()
    value = gr[0]
    for k in range(1, n_rad):
        value = value + gr[k]
    gtot[...] = value
    for k in range(1, n_rad):
        wire.copy(s4, share.at[(rad + n_rad - k) % n_rad], s_a + k, rad=rad).wait_recv()
    for copy in list(core.values()) + list(xs.values()) + list(zs.values()) + list(g_zs.values()):
        copy.wait_send()
    for copy in outs + g_outs + finals + [g_core, g_x]:
        copy.wait_send()


class Runs:
    def __init__(self):
        self.live = []

    def add(self, run):
        next(run)
        self.live.append(run)
        return run

    def tick(self, *runs):
        for run in runs:
            if run in self.live and next(run, self) is self:
                self.live.remove(run)

    def finish(self, *runs):
        while any(run in self.live for run in runs):
            self.tick(*runs)


COPIES = 192
GROUPS = 2
VM = pl.BlockSpec(memory_space=pltpu.VMEM)
SM = pl.BlockSpec(memory_space=pltpu.SMEM)
ANY = pl.BlockSpec(memory_space=pl.ANY)


def layer_kernel(n_rad, n_azi, shear, shift, tok, cot, gain_ref, wqkv_own, wout_own,
                 block_out, grad_out, share, gtot,
                 ext, main, far, w_own, w_all, cur, got, five, stage, cur_b, got_b, five_b, stage_b,
                 frame, acc, gsum, qkv_t, dat_t, att_t, dqkv_t,
                 low, r1, r2, s1, s2, r3, s3, r4, s4, gbuf, gz, gr, send, recv):
    wire = Wire(send, recv)
    rad, azi = wire.rad, wire.azi
    rows, cols, depth, width = tok.shape
    srcs = (tok, cot)
    n = WR * WA * depth
    before, after = (azi + n_azi - 1) % n_azi, (azi + 1) % n_azi
    middle, left, right = pl.ds(SIDE, cols), pl.ds(0, SIDE), pl.ds(cols + SIDE, SIDE)
    s_local = wire.slot(4)
    here = [
        wire.local(wqkv_own, w_own.at[:, pl.ds(0, 3 * width)], s_local),
        wire.local(wout_own, w_own.at[:, pl.ds(3 * width, width)], s_local + 1),
        wire.local(tok, main.at[0, :, middle], s_local + 2),
        wire.local(cot, main.at[1, :, middle], s_local + 3),
    ]
    for copy in here:
        copy.start()
    shift_rad, shift_azi = shift[0], shift[1]
    total_cols = cols * n_azi
    lean = jnp.where(shift_azi > SIDE, shift_azi - WA, shift_azi)
    forth = lax.rem(shear[0] + lean + total_cols, jnp.int32(total_cols))
    back = lax.rem(total_cols - forth, jnp.int32(total_cols))

    acc[...] = jnp.zeros_like(acc)
    gsum[...] = jnp.zeros_like(gsum)
    greet(n_rad, n_azi)
    for copy in here[:2]:
        copy.wait()

    runs = Runs()
    weights = runs.add(gather_weights(wire, w_own, w_all.at[...]))
    s_side = wire.slot(4)
    sides = []
    for t in range(2):
        sides.append(wire.copy(srcs[t].at[:, pl.ds(0, SIDE)], main.at[t, :, right],
                               s_side + 2 * t, azi=before))
        sides.append(wire.copy(srcs[t].at[:, pl.ds(cols - SIDE, SIDE)], main.at[t, :, left],
                               s_side + 2 * t + 1, azi=after))
    for copy in sides:
        copy.start()
    quarters = n_rad // 2
    come = (
        runs.add(roll(
            wire,
            lambda g: srcs[g // quarters].at[pl.ds(0, RIM), :, :, lane_block(g % quarters)],
            0, n_rad - 1, forth,
            lambda t, f: far.at[t, :, pl.ds(0, cols), :, lane_block(f)],
            cur, got, five, stage, n_rad, n_azi)),
        runs.add(rims(wire, lambda t: srcs[t].at[pl.ds(0, RIM)], far, 0, n_rad - 1, -1, cols,
                      n_rad, n_azi)),
    )
    step = 0
    while weights in runs.live:
        runs.tick(weights)
        if step % 2 == 1:
            runs.tick(come[0])
        step += 1
    for copy in here[2:]:
        copy.wait()
    for copy in sides:
        copy.wait()

    gain = gain_ref[...]
    deep = w_own.shape[0]
    wqkv = w_all.reshape(n_azi * deep, 4 * width).at[:, pl.ds(0, 3 * width)]
    wout = w_all.reshape(n_azi * deep, 4 * width).at[:, pl.ds(3 * width, width)]
    scale = HD ** -0.5
    col_near = SIDE + lean
    col_far = jnp.where(rad == n_rad - 1, 0, col_near)

    def line(t, i, j, r):
        row = shift_rad + WR * i + r
        near = main[t, jnp.minimum(row, rows - 1), pl.ds(col_near + WA * j, WA)].astype(F32)
        if WR * i + r + RIM < rows:
            return near
        other = far[t, jnp.maximum(row - rows, 0), pl.ds(col_far + WA * j, WA)].astype(F32)
        if WR * i + r + 1 >= rows:
            return other
        return jnp.where(row < rows, near, other)

    def window(i, j, *plan):
        def load(t):
            return jnp.concatenate(
                [line(t, i, j, r).reshape(WA * depth, width) for r in range(WR)], axis=0)

        x = load(0)
        g = load(1)
        centred = x - jnp.mean(x, axis=1, keepdims=True)
        inv = lax.rsqrt(jnp.mean(centred * centred, axis=1, keepdims=True) + EPS)
        xhat = centred * inv
        hidden = (xhat * gain).astype(BF16)
        g_low = g.astype(BF16)
        qkv_t[...] = mm(hidden, wqkv[...]).T.astype(BF16)
        dat_t[...] = mm(g_low, wout[...], NT).T.astype(BF16)

        def head(h, carry):
            at = pl.multiple_of(h * HD, HD)
            q = qkv_t[pl.ds(at, HD), :]
            k = qkv_t[pl.ds(width + at, HD), :]
            v = qkv_t[pl.ds(2 * width + at, HD), :]
            d = dat_t[pl.ds(at, HD), :]
            s = mm(k, q, TN)
            e = jnp.exp2((s - jnp.max(s, axis=0, keepdims=True)) * (scale * LOG2E))
            p = e * (1.0 / jnp.sum(e, axis=0, keepdims=True))
            low_p = p.astype(BF16)
            att = mm(v, low_p)
            att_t[pl.ds(at, HD), :] = att.astype(BF16)
            dp = mm(v, d, TN)
            dot = jnp.sum(att * d.astype(F32), axis=0, keepdims=True)
            ds = (p * (dp - dot)).astype(BF16)
            dqkv_t[pl.ds(at, HD), :] = (mm(k, ds) * scale).astype(BF16)
            dqkv_t[pl.ds(width + at, HD), :] = (mm(q, ds, NT) * scale).astype(BF16)
            dqkv_t[pl.ds(2 * width + at, HD), :] = mm(d, low_p, NT).astype(BF16)
            return carry

        each = HEADS // GROUPS
        for group in range(GROUPS):
            lax.fori_loop(group * each, (group + 1) * each, head, 0, unroll=UNROLL)
            runs.tick(*(plan[group] if plan else ()))
        shape = (WR, WA, depth, width)
        own, at = pl.ds(WR * i, WR), pl.ds(WA * j, WA)
        att_all = att_t[...]
        frame[0, own, at] = (x + mm(att_all, wout[...], TN)).reshape(shape).astype(BF16)
        dqkv = dqkv_t[...]
        acc[:, : 3 * width] += mm(hidden, dqkv, TT)
        acc[:, 3 * width:] += mm(att_all, g_low)
        dh = mm(dqkv, wqkv[...], TT)
        gsum[...] += jnp.sum(dh * xhat, axis=0, keepdims=True)
        dx = dh * gain
        dx = inv * (dx - jnp.mean(dx, axis=1, keepdims=True)
                    - xhat * jnp.mean(dx * xhat, axis=1, keepdims=True))
        frame[1, own, at] = (g + dx).reshape(shape).astype(BF16)

    s_out = wire.slot(8)
    back_sides = {}
    for i in range(2):
        own = pl.ds(WR * i, WR)
        there = pl.ds(RIM + WR * i, WR)
        back_sides[i, 0] = wire.copy(frame.at[:, own, pl.ds(0, SIDE)], ext.at[:, there, right],
                                     s_out + 2 * i, azi=before)
        back_sides[i, 1] = wire.copy(frame.at[:, own, pl.ds(cols - SIDE, SIDE)],
                                     ext.at[:, there, left], s_out + 2 * i + 1, azi=after)
    window(0, 0, come[:1], come)
    back_sides[0, 0].start()
    runs.finish(*come)
    window(1, 0)
    window(1, 1)
    go = (
        runs.add(roll(
            wire,
            lambda g: frame.at[g // quarters, pl.ds(rows - RIM, RIM), :, :,
                               lane_block(g % quarters)],
            n_rad - 1, 0, back,
            lambda t, f: ext.at[t, pl.ds(0, RIM), pl.ds(0, cols), :, lane_block(f)],
            cur_b, got_b, five_b, stage_b, n_rad, n_azi)),
        runs.add(rims(wire, lambda t: frame.at[t, pl.ds(rows - RIM, RIM)],
                      ext.at[:, pl.ds(0, RIM)], n_rad - 1, 0, 1, cols, n_rad, n_azi)),
    )
    back_sides[1, 0].start()
    back_sides[1, 1].start()
    window(0, 1, go[:1], go[:1])
    back_sides[0, 1].start()
    final = [wire.local(frame.at[t], ext.at[t, pl.ds(RIM, rows), middle], s_out + 4 + t)
             for t in range(2)]
    for copy in final:
        copy.start()
    sums = runs.add(sum_weights(wire, acc, low, gsum, share, gtot, r1, r2, s1, s2, r3, s3, r4, s4, gbuf,
                         gz, gr, n_rad))
    step = 0
    while sums in runs.live:
        runs.tick(sums)
        if step % 2 == 1:
            runs.tick(*go[:1 + step // 3])
        step += 1
    runs.finish(*go)
    for copy in list(back_sides.values()) + final:
        copy.wait()
    outer = SIDE - lean
    above = jnp.where(rad == 0, 0, outer)
    for t, ref in enumerate((block_out, grad_out)):
        for r in range(rows):
            row = RIM - shift_rad + r
            first = jnp.where(row < RIM, above, outer)
            ref[r] = ext[t, row, pl.ds(first, cols)]


def layer(shear, shift, tok, cot, gain, wqkv, wout, n_rad, n_azi):
    rows, cols, depth, width = tok.shape
    deep, wide = wout.shape[0], 4 * width
    part = wide // n_rad
    n = WR * WA * depth
    across = cols + 2 * SIDE

    def kernel(*refs):
        layer_kernel(n_rad, n_azi, *refs)

    rolls = [
        pltpu.VMEM((2, RIM, cols, depth, LANES), BF16),
        pltpu.VMEM((4, RIM, cols, depth, LANES), BF16),
        pltpu.VMEM((RIM, 5 * cols, depth, LANES), BF16),
        pltpu.VMEM((RIM, cols, depth, LANES), BF16),
    ]
    return pl.pallas_call(
        kernel,
        out_shape=(
            jax.ShapeDtypeStruct(tok.shape, BF16),
            jax.ShapeDtypeStruct(tok.shape, BF16),
            jax.ShapeDtypeStruct((n_rad, deep, part), BF16),
            jax.ShapeDtypeStruct((1, width), F32),
        ),
        in_specs=[SM, SM, ANY, ANY, VM, ANY, ANY],
        out_specs=(VM, VM, VM, VM),
        scratch_shapes=[
            pltpu.VMEM((2, rows + RIM, across, depth, width), BF16),
            pltpu.VMEM((2, rows, across, depth, width), BF16),
            pltpu.VMEM((2, RIM, across, depth, width), BF16),
            pltpu.VMEM((deep, wide), BF16),
            pltpu.VMEM((n_azi, deep, wide), BF16),
        ] + rolls + rolls + [
            pltpu.VMEM((2, rows, cols, depth, width), BF16),
            pltpu.VMEM((width, wide), F32),
            pltpu.VMEM((1, width), F32),
            pltpu.VMEM((3 * width, n), BF16),
            pltpu.VMEM((width, n), BF16),
            pltpu.VMEM((width, n), BF16),
            pltpu.VMEM((3 * width, n), BF16),
            pltpu.VMEM((NX, NZ, deep, wide), BF16),
            pltpu.VMEM((NX, NZ, deep, wide), BF16),
            pltpu.VMEM((NZ, deep, wide), BF16),
            pltpu.VMEM((NZ, deep, wide), BF16),
            pltpu.VMEM((NZ, deep, wide), BF16),
            pltpu.VMEM((NZ, deep, wide), BF16),
            pltpu.VMEM((n_rad, deep, part), BF16),
            pltpu.VMEM((n_rad, deep, part), BF16),
            pltpu.VMEM((deep, part), BF16),
            pltpu.VMEM((3, 1, width), F32),
            pltpu.VMEM((NZ, 1, width), F32),
            pltpu.VMEM((n_rad, 1, width), F32),
            pltpu.SemaphoreType.DMA((COPIES,)),
            pltpu.SemaphoreType.DMA((COPIES,)),
        ],
        compiler_params=pltpu.CompilerParams(
            collective_id=0, has_side_effects=True, vmem_limit_bytes=VMEM_LIMIT),
    )(shear, shift, tok, cot, gain, wqkv, wout)


def on_device(tokens, cotangent, ln_gain, qkv_weight, out_weight, shear_offset, window_shift):
    rows, cols, depth, width = tokens.shape
    n_rad, n_azi = lax.axis_size("rad"), lax.axis_size("azi")
    block_out, grad_tokens, share, gtot = layer(
        shear_offset, window_shift, tokens, cotangent, ln_gain.reshape(1, width), qkv_weight,
        out_weight, n_rad, n_azi)
    factor = float(rows * cols * depth * n_rad * n_azi) ** (-0.5)
    share = share.transpose(1, 0, 2).reshape(width // n_azi, 4 * width).astype(F32) * factor
    return (block_out, grad_tokens, share[:, : 3 * width], share[:, 3 * width:],
            gtot.reshape(width) * factor)


def solution(mesh):
    in_specs = (
        P("rad", "azi", None, None),
        P("rad", "azi", None, None),
        P(),
        P("azi", None),
        P("azi", None),
        P(),
        P(),
    )
    out_specs = (
        P("rad", "azi", None, None),
        P("rad", "azi", None, None),
        P("azi", None),
        P("azi", None),
        P(),
    )
    return jax.shard_map(
        on_device, mesh=mesh, in_specs=in_specs, out_specs=out_specs, check_vma=False
    )
```
